512 devices in a mesh: lat: 32 (over z, x_lo), lon: 16 (over y, x_hi, core).
Axes of the slice: x: 4 (x_hi: 2, x_lo: 2; x = x_hi * 2 + x_lo), y: 4, z: 16, core: 2. Of those that a mesh axis runs over, the one named last changes fastest.
Arguments:
- observed: float32 [4096, 8192], P(('lat', 'lon')), may hold values from -12 to 12
- gauged: int32 [4096, 8192], P('lat', 'lon'), may hold values from 0 to 1, as said below
Outputs:
- coarsest_coeffs: float32 [512, 1024], P('lat', 'lon')
- coarse_coeffs: float32 [1024, 2048], P('lat', 'lon')
- fine_coeffs: float32 [2048, 4096], P('lat', 'lon')
- finest_coeffs: float32 [4096, 8192], P('lat', 'lon')
- imputed: float32 [4096, 8192], P(('lat', 'lon'))
The draws below stay inside these ranges and needn't reach their ends.
Inputs may be any that keep to these rules, and one draw needn't show every extreme that they name: 1 marks a gauged cell.
All inputs are finite; a program needn't handle non-finite values.
Results may differ from the reference program's by a relative error of at most 0.00029.
Values sent between devices are 32-bit elements; how exact they have to be, the bound alone decides.
A program may use at most 64 MiB of HBM per device.

```python
import math
import jax
import jax.numpy as jnp
from jax import lax

LEVELS = 4
ITERS = 2
NLAT = 4096
NLON = 8192


def draw_observed(key, part):
    lon_frac = jnp.arange(NLON, dtype=jnp.float32)[None, :] / NLON
    amplitude = 0.3 * jnp.exp(jnp.log(10.0) * lon_frac)
    rough = jnp.clip(jax.random.normal(key, (NLAT, NLON), jnp.float32), -4.0, 4.0)
    return rough * amplitude


def draw_gauged(key, part):
    row_index = jnp.arange(NLAT, dtype=jnp.int32)[:, None]
    threshold = 200 + 600 * row_index // NLAT
    drawn = jax.random.randint(key, (NLAT, NLON), 0, 1000, dtype=jnp.int32)
    return (drawn < threshold).astype(jnp.int32)


def setup_inputs(seed: int = 0) -> dict:
    key_of = jax.random.split(jax.random.key(seed), 3)
    observed = draw_observed(jax.random.fold_in(key_of[2], 71), 0)
    gauged = draw_gauged(jax.random.fold_in(key_of[2], 71), 0)
    return {"observed": observed, "gauged": gauged}


highest = lax.Precision.HIGHEST
data_weight = 2.0
kappa_term = 5.0
level_scales = (0.02, 0.03, 0.05, 0.08)

def wendland(distance):
    remain = jnp.maximum(1.0 - distance, 0.0)
    return remain ** 6 * (35.0 * distance * distance + 18.0 * distance + 3.0) / 3.0

def weights_table(spacing):
    offsets = jnp.arange(spacing, dtype=jnp.int32)[:, None]
    shifts = jnp.arange(5, dtype=jnp.int32)[None, :] - 2
    numerator = jnp.abs(2 * offsets - 2 * spacing * shifts - (spacing - 1))
    return wendland(numerator.astype(jnp.float32) / (5.0 * spacing)) / math.sqrt(spacing)

def spread(coeffs, table, spacing):
    node_count = coeffs.shape[0]
    padded = jnp.pad(coeffs, ((2, 2), (0, 0)))
    result = jnp.zeros((node_count, spacing, coeffs.shape[1]), jnp.float32)
    for offset in range(5):
        result = result + table[:, offset][None, :, None] * padded[offset:offset + node_count][:, None, :]
    return result.reshape(node_count * spacing, coeffs.shape[1])

def collect(surface, table, spacing):
    node_count = surface.shape[0] // spacing
    blocks = surface.reshape(node_count, spacing, surface.shape[1])
    accum = jnp.zeros((node_count, surface.shape[1]), jnp.float32)
    for offset in range(5):
        summed = jnp.einsum('ntm,t->nm', blocks, table[:, offset], precision=highest)
        padded = jnp.pad(summed, ((2, 2), (0, 0)))
        accum = accum + padded[4 - offset:4 - offset + node_count]
    return accum

def synthesize(coeffs, spacings):
    surface = jnp.zeros((NLAT, NLON), jnp.float32)
    for level_idx in range(LEVELS):
        spacing = spacings[level_idx]
        table = weights_table(spacing)
        row_part = spread(coeffs[level_idx], table, spacing)
        surface = surface + spread(row_part.T, table, spacing).T
    return surface

def adjoint_all(misfit, spacings):
    result = []
    for level_idx in range(LEVELS):
        spacing = spacings[level_idx]
        table = weights_table(spacing)
        row_part = collect(misfit, table, spacing)
        result.append(collect(row_part.T, table, spacing).T)
    return result

def autoreg(coeffs):
    padded = jnp.pad(coeffs, 1)
    beside = padded[2:, 1:-1] + padded[:-2, 1:-1] + padded[1:-1, 2:] + padded[1:-1, :-2]
    return kappa_term * coeffs - beside

def apply_operator(coeffs, gauge_float, spacings):
    surface = synthesize(coeffs, spacings)
    backs = adjoint_all(data_weight * gauge_float * surface, spacings)
    curv_sum = data_weight * jnp.sum(gauge_float * surface * surface)
    images = []
    for level_idx in range(LEVELS):
        smoothed = autoreg(coeffs[level_idx])
        images.append(backs[level_idx] + level_scales[level_idx] * autoreg(smoothed))
        curv_sum = curv_sum + level_scales[level_idx] * jnp.sum(smoothed * smoothed)
    return (images, curv_sum)

def level_products(first, second):
    accum = jnp.float32(0.0)
    for level_idx in range(LEVELS):
        accum = accum + jnp.sum(first[level_idx] * second[level_idx])
    return accum

def reference(observed, gauged):
    spacings = [2 ** (LEVELS - 1 - level_idx) for level_idx in range(LEVELS)]
    gauge_float = gauged.astype(jnp.float32)
    right_side = adjoint_all(data_weight * gauge_float * observed, spacings)
    solution = [jnp.zeros_like(part_now) for part_now in right_side]
    residual = right_side
    search = right_side
    res_norm = level_products(residual, residual)
    for iteration in range(ITERS):
        images, curv_sum = apply_operator(search, gauge_float, spacings)
        step_size = res_norm / curv_sum
        solution = [solution[k] + step_size * search[k] for k in range(LEVELS)]
        if iteration + 1 < ITERS:
            residual = [residual[k] - step_size * images[k] for k in range(LEVELS)]
            new_norm = level_products(residual, residual)
            search = [residual[k] + new_norm / res_norm * search[k] for k in range(LEVELS)]
            res_norm = new_norm
    imputed = synthesize(solution, spacings)
    return (solution[0], solution[1], solution[2], solution[3], imputed)
```

```python
import functools
import math

import jax
import jax.numpy as jnp
import numpy as np
from jax import lax
from jax.experimental import pallas as pl
from jax.experimental.pallas import tpu as pltpu
from jax.sharding import PartitionSpec as P

LEVELS = 4
SPACINGS = (8, 4, 2, 1)
SCALES = (0.02, 0.03, 0.05, 0.08)
HALO = 64
MARGIN = 4
MESH = pl.DeviceIdType.MESH
F32 = jnp.float32
BF16 = jnp.bfloat16


def weight(cells, nodes, spacing):
    numerator = np.abs(2 * cells - 2 * spacing * nodes - (spacing - 1))
    d = numerator / (5.0 * spacing)
    value = np.maximum(1.0 - d, 0.0) ** 6 * (35.0 * d * d + 18.0 * d + 3.0) / 3.0
    return value / math.sqrt(spacing)


def halves(table):
    table = np.asarray(table, np.float32)
    high = table.astype(BF16)
    low = (table - high.astype(np.float32)).astype(BF16)
    return jnp.asarray(high), jnp.asarray(low)


def lanes_of(width, spacing):
    return -(-(width // spacing) // 128) * 128


def tables(rows, cols):
    width = cols + 2 * HALO
    row_parts, col_parts = [], []
    for s in SPACINGS[:3]:
        nodes = np.arange(rows // s + 2 * MARGIN) - MARGIN
        row_parts.append(weight(np.arange(rows)[None, :], nodes[:, None], s))
        nodes = np.arange(width // s) - HALO // s
        part = np.zeros((width, lanes_of(width, s)))
        part[:, : width // s] = weight(np.arange(width)[:, None] - HALO, nodes[None, :], s)
        col_parts.append(part)
    back = np.concatenate(row_parts, axis=0)
    spread = np.zeros((rows, -(-back.shape[0] // 16) * 16))
    spread[:, : back.shape[0]] = back.T
    return (*halves(back), *halves(spread), *halves(np.concatenate(col_parts, axis=1)))


def split(x):
    high = x.astype(BF16)
    return high, (x - high.astype(F32)).astype(BF16)


def dot(a, b):
    return jnp.dot(a, b, preferred_element_type=F32)


def dot_t(a, b):
    return lax.dot_general(a, b, (((1,), (1,)), ((), ())), preferred_element_type=F32)


def roll(x, shift, axis):
    return pltpu.roll(x, shift % x.shape[axis], axis)


TAPS = [float(np.float32(weight(np.int64(0), np.int64(o), 1))) for o in range(3)]


def five(x, axis):
    near = roll(x, 1, axis) + roll(x, -1, axis)
    far = roll(x, 2, axis) + roll(x, -2, axis)
    return TAPS[0] * x + TAPS[1] * near + TAPS[2] * far


def stencil(x):
    return 5.0 * x - (roll(x, 1, 0) + roll(x, -1, 0) + roll(x, 1, 1) + roll(x, -1, 1))


def total(x):
    return jnp.sum(jnp.sum(x, axis=0, keepdims=True), axis=1, keepdims=True)


def kernel(n_lat, n_lon, *refs):
    (
        obs_ref, gau_ref, back_h, back_l, spread_h, spread_l, cols_h_hbm, cols_l_hbm,
        r0_out, r1_out, r2_out, r3_out, q0_out, q1_out, q2_out, q3_out, first_out, second_out, mix_out,
        cols_h, cols_l, obs_pad, obs_tile, gau_pad, gau_left, gau_right, extended,
        up_send, down_send, from_up, from_down, swath_src, swath_dst, red_src, red_lon, red_lat,
        table_sem, obs_sem, gau_sem, strip_sem, swath_sem, lon_sem, lat_sem,
    ) = refs
    r_out = (r0_out, r1_out, r2_out, r3_out)
    q_out = (q0_out, q1_out, q2_out, q3_out)
    lat, lon = lax.axis_index("lat"), lax.axis_index("lon")
    rows, cols = gau_ref.shape
    width = cols + 2 * HALO
    swath = obs_ref.shape[0]
    lanes = [lanes_of(width, s) for s in SPACINGS]
    starts = [sum(lanes[:k]) for k in range(LEVELS)]
    heights = [rows // s + 2 * MARGIN for s in SPACINGS]
    tops = [sum(heights[:k]) for k in range(LEVELS)]

    def lon_peer(d):
        return lax.rem(lon + d, n_lon)

    def lat_peer(d):
        return lax.rem(lat + d, n_lat)

    load_h = pltpu.make_async_copy(cols_h_hbm, cols_h, table_sem.at[0])
    load_l = pltpu.make_async_copy(cols_l_hbm, cols_l, table_sem.at[1])
    load_h.start()
    load_l.start()

    barrier = pltpu.get_barrier_semaphore()

    def greet_lon(d, c):
        pl.semaphore_signal(barrier, inc=1, device_id={"lon": lon_peer(d)}, device_id_type=MESH)
        return c

    def greet_lat(d, c):
        pl.semaphore_signal(barrier, inc=1, device_id={"lat": lat_peer(d)}, device_id_type=MESH)
        return c

    lax.fori_loop(1, n_lat, greet_lat, 0)
    lax.fori_loop(1, n_lon, greet_lon, 0)

    obs_pad[:, :128] = jnp.zeros((swath, 128), F32)
    obs_pad[:, n_lon * cols :] = jnp.zeros((swath, 128), F32)
    obs_pad[:, HALO : HALO + n_lon * cols] = obs_ref[...]
    gau_pad[:, :128] = jnp.zeros((rows, 128), F32)
    gau_pad[:, cols:] = jnp.zeros((rows, 128), F32)
    gau_pad[:, HALO : HALO + cols] = gau_ref[...].astype(F32)
    extended[...] = jnp.zeros_like(extended)

    pl.semaphore_wait(barrier, n_lat - 1 + n_lon - 1)

    def scatter(d, c):
        peer = lon_peer(d)
        pltpu.make_async_remote_copy(
            src_ref=obs_pad.at[:, pl.ds(pl.multiple_of(peer * cols, 128), width)],
            dst_ref=obs_tile.at[pl.ds(pl.multiple_of(lon * swath, 8), swath), :],
            send_sem=obs_sem.at[0],
            recv_sem=obs_sem.at[1],
            device_id={"lon": peer},
            device_id_type=MESH,
        ).start()
        return c

    def beside(src, dst, which, d):
        return pltpu.make_async_remote_copy(
            src_ref=src,
            dst_ref=dst,
            send_sem=gau_sem.at[2 * which],
            recv_sem=gau_sem.at[2 * which + 1],
            device_id={"lon": lon_peer(d)},
            device_id_type=MESH,
        )

    to_right = beside(gau_pad.at[:, cols:], gau_left, 0, 1)
    to_left = beside(gau_pad.at[:, :128], gau_right, 1, n_lon - 1)
    lax.fori_loop(1, n_lon, scatter, 0)
    to_right.start()
    to_left.start()
    own = pl.ds(pl.multiple_of(lon * swath, 8), swath)
    obs_tile[own, :] = obs_pad[:, pl.ds(pl.multiple_of(lon * cols, 128), width)]

    load_h.wait()
    load_l.wait()
    to_right.wait()
    to_left.wait()
    gau_pad[:, :128] += gau_left[...] * jnp.where(lon > 0, 1.0, 0.0)
    gau_pad[:, cols:] += gau_right[...] * jnp.where(lon < n_lon - 1, 1.0, 0.0)
    all_obs = obs_tile.at[: (n_lon - 1) * swath]
    pltpu.make_async_copy(all_obs, all_obs, obs_sem.at[1]).wait()
    pltpu.make_async_copy(all_obs, all_obs, obs_sem.at[0]).wait()

    valid = []
    inside = []
    for k, s in enumerate(SPACINGS):
        row = lax.broadcasted_iota(jnp.int32, (heights[k], 1), 0) - MARGIN
        col = lax.broadcasted_iota(jnp.int32, (1, lanes[k]), 1) - HALO // s
        row_global, col_global = row + lat * (rows // s), col + lon * (cols // s)
        row_ok = jnp.where((row_global >= 0) & (row_global < n_lat * (rows // s)), 1.0, 0.0)
        col_ok = jnp.where((col_global >= 0) & (col_global < n_lon * (cols // s)), 1.0, 0.0)
        valid.append(row_ok * col_ok)
        row_own = jnp.where((row >= 0) & (row < rows // s), 1.0, 0.0)
        col_own = jnp.where((col >= 0) & (col < cols // s), 1.0, 0.0)
        inside.append((row_own, col_own))

    def columns(k):
        at = slice(starts[k], starts[k] + lanes[k])
        return cols_h[:, at], cols_l[:, at]

    def adjoint(misfit):
        high, low = split(misfit)
        part = dot(back_h[...], high) + dot(back_h[...], low) + dot(back_l[...], high)
        result = []
        for k in range(3):
            high, low = split(part[tops[k] : tops[k] + heights[k]])
            table_h, table_l = columns(k)
            result.append(dot(high, table_h) + dot(high, table_l) + dot(low, table_h))
        extended[MARGIN : MARGIN + rows, :] = five(misfit, 1)
        result.append(five(extended[...], 0))
        return result

    def forward(coeffs):
        parts = []
        for k in range(3):
            high, low = split(coeffs[k])
            table_h, table_l = columns(k)
            parts.append(dot_t(high, table_h) + dot_t(high, table_l) + dot_t(low, table_h))
        fill = spread_h.shape[1] - sum(heights[:3])
        if fill:
            parts.append(jnp.zeros((fill, width), F32))
        high, low = split(jnp.concatenate(parts, axis=0))
        coarse = dot(spread_h[...], high) + dot(spread_h[...], low) + dot(spread_l[...], high)
        fine = five(coeffs[3], 0)[MARGIN : MARGIN + rows]
        return coarse + five(fine, 1)

    def strips(which, partial):
        for k in range(LEVELS):
            at = slice(starts[k], starts[k] + lanes[k])
            up_send[which, :, at] = partial[k][:8]
            down_send[which, :, at] = partial[k][heights[k] - 8 :]
        copies = []
        for j, (src, dst, d) in enumerate(((up_send, from_down, n_lat - 1), (down_send, from_up, 1))):
            copies.append(
                pltpu.make_async_remote_copy(
                    src_ref=src.at[which],
                    dst_ref=dst.at[which],
                    send_sem=strip_sem.at[4 * which + 2 * j],
                    recv_sem=strip_sem.at[4 * which + 2 * j + 1],
                    device_id={"lat": lat_peer(d)},
                    device_id_type=MESH,
                )
            )
            copies[-1].start()
        return copies

    def joined(which, partial):
        result = []
        has_up = jnp.where(lat > 0, 1.0, 0.0)
        has_down = jnp.where(lat < n_lat - 1, 1.0, 0.0)
        for k in range(LEVELS):
            at = slice(starts[k], starts[k] + lanes[k])
            head = partial[k][:8] + has_up * from_up[which, :, at]
            tail = partial[k][heights[k] - 8 :] + has_down * from_down[which, :, at]
            middle = partial[k][8 : heights[k] - 8]
            result.append(jnp.concatenate([head, middle, tail], axis=0) * valid[k])
        return result

    def send_swaths(which, surface):
        swath_src[which] = surface[:, HALO : HALO + cols]

        def push(d, c):
            peer = lon_peer(d)
            pltpu.make_async_remote_copy(
                src_ref=swath_src.at[which, pl.ds(pl.multiple_of(peer * swath, 8), swath), :],
                dst_ref=swath_dst.at[which, :, pl.ds(pl.multiple_of(lon * cols, 128), cols)],
                send_sem=swath_sem.at[2 * which],
                recv_sem=swath_sem.at[2 * which + 1],
                device_id={"lon": peer},
                device_id_type=MESH,
            ).start()
            return c

        lax.fori_loop(1, n_lon, push, 0)
        at = pl.ds(pl.multiple_of(lon * cols, 128), cols)
        swath_dst[which, :, at] = swath_src[which, own, :]

    def extract(k, x):
        s = SPACINGS[k]
        return x[MARGIN : MARGIN + rows // s, HALO // s : HALO // s + cols // s]

    def squares(k, x):
        row_own, col_own = inside[k]
        return total(x * x * row_own * col_own)

    lane = lax.broadcasted_iota(jnp.int32, (1, width), 1)
    own_lane = jnp.where((lane >= HALO) & (lane < HALO + cols), 1.0, 0.0)
    gauge = gau_pad[...]

    partial = adjoint(2.0 * gauge * obs_tile[...])
    copies = strips(0, partial)
    for copy in copies:
        copy.wait()
    right = joined(0, partial)

    surface = forward(right)
    misfit = 2.0 * gauge * surface
    partial = adjoint(misfit)
    copies = strips(1, partial)
    send_swaths(0, surface)
    mu0 = jnp.zeros((1, 1), F32)
    mu1 = total(misfit * surface * own_lane)
    rough = []
    for k in range(LEVELS):
        smooth = stencil(right[k]) * valid[k]
        rough.append(SCALES[k] * stencil(smooth) * valid[k])
        mu0 = mu0 + squares(k, right[k])
        mu1 = mu1 + SCALES[k] * squares(k, smooth)
        r_out[k][...] = extract(k, right[k])
    for copy in copies:
        copy.wait()
    image = [x + y for x, y in zip(joined(1, partial), rough)]

    surface = forward(image)
    mu2 = jnp.zeros((1, 1), F32)
    mu3 = total(2.0 * gauge * surface * surface * own_lane)
    for k in range(LEVELS):
        mu2 = mu2 + squares(k, image[k])
        mu3 = mu3 + SCALES[k] * squares(k, stencil(image[k]) * valid[k])

    def placed(values):
        at = lax.broadcasted_iota(jnp.int32, (1, 128), 1)
        row = jnp.zeros((1, 128), F32)
        for i, value in enumerate(values):
            row = row + jnp.where(at == i, value, 0.0)
        return row

    def reduce_start(stage, value, dst, sem, count, axis, peer_of):
        red_src[stage] = value

        def push(d, c):
            pltpu.make_async_remote_copy(
                src_ref=red_src.at[stage],
                dst_ref=dst.at[d - 1],
                send_sem=sem.at[0],
                recv_sem=sem.at[1],
                device_id={axis: peer_of(d)},
                device_id_type=MESH,
            ).start()
            return c

        lax.fori_loop(1, count, push, 0)

    def reduce_end(value, dst, sem):
        pltpu.make_async_copy(dst, dst, sem.at[1]).wait()
        pltpu.make_async_copy(dst, dst, sem.at[0]).wait()
        return value + jnp.sum(dst[...], axis=0)

    moments = placed((mu0, mu1, mu2, mu3))
    reduce_start(0, moments, red_lon, lon_sem, n_lon, "lon", lon_peer)
    send_swaths(1, surface)
    for k in range(LEVELS):
        q_out[k][...] = extract(k, image[k])
    moments = reduce_end(moments, red_lon, lon_sem)
    reduce_start(1, moments, red_lat, lat_sem, n_lat, "lat", lat_peer)
    moments = reduce_end(moments, red_lat, lat_sem)

    m0, m1, m2, m3 = (moments[:, i : i + 1] for i in range(4))
    alpha = m0 / m1
    grow = alpha * m2 / m1
    second_norm = alpha * alpha * m2 - m0
    curv = alpha * alpha * m3 - grow * grow * m1
    gamma = second_norm / curv
    mix_out[...] = placed((alpha + gamma * grow, -alpha * gamma))

    everything = swath_dst.at[0, :, : (n_lon - 1) * cols]
    for i in range(4):
        pltpu.make_async_copy(everything, everything, swath_sem.at[i]).wait()
    first_out[...] = swath_dst[0]
    second_out[...] = swath_dst[1]


def combine(*refs):
    mix = refs[0][...]
    a, b = mix[:, 0:1], mix[:, 1:2]
    count = LEVELS + 1
    for first, second, out in zip(refs[1 : 1 + count], refs[1 + count : 1 + 2 * count], refs[1 + 2 * count :]):
        out[...] = a * first[...] + b * second[...]


def body(observed, gauged):
    n_lat, n_lon = lax.axis_size("lat"), lax.axis_size("lon")
    rows, cols = gauged.shape
    swath = observed.shape[0]
    width = cols + 2 * HALO
    back_h, back_l, spread_h, spread_l, cols_h, cols_l = tables(rows, cols)
    level_shapes = [jax.ShapeDtypeStruct((rows // s, cols // s), F32) for s in SPACINGS]
    swath_shape = jax.ShapeDtypeStruct(observed.shape, F32)
    strip = 8 * sum(lanes_of(width, s) for s in SPACINGS)
    vmem = pl.BlockSpec(memory_space=pltpu.VMEM)
    anywhere = pl.BlockSpec(memory_space=pl.ANY)
    dma = pltpu.SemaphoreType.DMA
    *pieces, mix = pl.pallas_call(
        functools.partial(kernel, n_lat, n_lon),
        out_shape=(
            *level_shapes,
            *level_shapes,
            swath_shape,
            swath_shape,
            jax.ShapeDtypeStruct((1, 128), F32),
        ),
        in_specs=[vmem] * 6 + [anywhere] * 2,
        out_specs=[vmem] * 11,
        scratch_shapes=[
            pltpu.VMEM(cols_h.shape, BF16),
            pltpu.VMEM(cols_l.shape, BF16),
            pltpu.VMEM((swath, n_lon * cols + 2 * HALO), F32),
            pltpu.VMEM((rows, width), F32),
            pltpu.VMEM((rows, width), F32),
            pltpu.VMEM((rows, 128), F32),
            pltpu.VMEM((rows, 128), F32),
            pltpu.VMEM((rows + 2 * MARGIN, width), F32),
            *[pltpu.VMEM((2, 8, strip // 8), F32)] * 4,
            pltpu.VMEM((2, rows, cols), F32),
            pltpu.VMEM((2, swath, n_lon * cols), F32),
            pltpu.VMEM((2, 1, 128), F32),
            pltpu.VMEM((n_lon - 1, 1, 128), F32),
            pltpu.VMEM((n_lat - 1, 1, 128), F32),
            dma((2,)),
            dma((2,)),
            dma((4,)),
            dma((8,)),
            dma((4,)),
            dma((2,)),
            dma((2,)),
        ],
        compiler_params=pltpu.CompilerParams(collective_id=0, has_side_effects=True),
        name="krylov",
    )(observed, gauged, back_h, back_l, spread_h, spread_l, cols_h, cols_l)
    firsts = [*pieces[:LEVELS], pieces[2 * LEVELS]]
    seconds = [*pieces[LEVELS : 2 * LEVELS], pieces[2 * LEVELS + 1]]
    return pl.pallas_call(
        combine,
        out_shape=(*level_shapes, swath_shape),
        in_specs=[vmem] * 11,
        out_specs=[vmem] * 5,
        name="combine",
    )(mix, *firsts, *seconds)


def solution(mesh):
    tile = P("lat", "lon")
    swaths = P(("lat", "lon"), None)
    return jax.shard_map(
        body,
        mesh=mesh,
        in_specs=(swaths, tile),
        out_specs=(tile, tile, tile, tile, swaths),
        check_vma=False,
    )
```

```python
import functools
import math

import jax
import jax.numpy as jnp
import numpy as np
from jax import lax
from jax.experimental import pallas as pl
from jax.experimental.pallas import tpu as pltpu
from jax.sharding import PartitionSpec as P

LEVELS = 4
SPACINGS = (8, 4, 2, 1)
SCALES = (0.02, 0.03, 0.05, 0.08)
HALO = 64
MARGIN = 4
MESH = pl.DeviceIdType.MESH
F32 = jnp.float32
BF16 = jnp.bfloat16


def weight(cells, nodes, spacing):
    numerator = np.abs(2 * cells - 2 * spacing * nodes - (spacing - 1))
    d = numerator / (5.0 * spacing)
    value = np.maximum(1.0 - d, 0.0) ** 6 * (35.0 * d * d + 18.0 * d + 3.0) / 3.0
    return value / math.sqrt(spacing)


def halves(table):
    table = np.asarray(table, np.float32)
    high = table.astype(BF16)
    low = (table - high.astype(np.float32)).astype(BF16)
    return jnp.asarray(np.concatenate([high, low], axis=0))


def lanes_of(width, spacing):
    return -(-(width // spacing) // 128) * 128


def tables(rows, cols):
    width = cols + 2 * HALO
    row_parts, col_parts = [], []
    for s in SPACINGS[:3]:
        nodes = np.arange(rows // s + 2 * MARGIN) - MARGIN
        row_parts.append(weight(np.arange(rows)[None, :], nodes[:, None], s))
        nodes = np.arange(width // s) - HALO // s
        part = np.zeros((width, lanes_of(width, s)))
        part[:, : width // s] = weight(np.arange(width)[:, None] - HALO, nodes[None, :], s)
        col_parts.append(part)
    back = np.concatenate(row_parts, axis=0)
    spread = np.zeros((rows, 128 * len(row_parts)))
    for k, part in enumerate(row_parts):
        spread[:, 128 * k : 128 * k + part.shape[0]] = part.T
    return halves(back), halves(spread), halves(np.concatenate(col_parts, axis=1))


def halve(x):
    high = x.astype(BF16).astype(F32)
    return jnp.concatenate([high, x - high], axis=0).astype(BF16)


def times(x, high, low, transposed=False):
    contract = (((1,), (1 if transposed else 0,)), ((), ()))
    n = x.shape[0]
    x = halve(x)
    both = lax.dot_general(x, high, contract, preferred_element_type=F32)
    rest = lax.dot_general(x[:n], low, contract, preferred_element_type=F32)
    return both[:n] + both[n:] + rest


def into(table, x):
    n = table.shape[0] // 2
    high = x.astype(BF16)
    low = (x - high.astype(F32)).astype(BF16)
    both = jnp.dot(table, high, preferred_element_type=F32)
    rest = jnp.dot(table[:n], low, preferred_element_type=F32)
    return both[:n] + both[n:] + rest


def roll(x, shift, axis):
    return pltpu.roll(x, shift % x.shape[axis], axis)


TAPS = [float(np.float32(weight(np.int64(0), np.int64(o), 1))) for o in range(3)]


def five(x, axis):
    near = roll(x, 1, axis) + roll(x, -1, axis)
    far = roll(x, 2, axis) + roll(x, -2, axis)
    return TAPS[0] * x + TAPS[1] * near + TAPS[2] * far


def stencil(x):
    return 5.0 * x - (roll(x, 1, 0) + roll(x, -1, 0) + roll(x, 1, 1) + roll(x, -1, 1))


def fold(x):
    return jnp.sum(x.reshape(x.shape[0] // 8, 8, x.shape[1]), axis=0)


def fold_lanes(x):
    result = x[:, :128]
    for at in range(128, x.shape[1], 128):
        result = result + x[:, at : at + 128]
    return result


def kernel(n_lat, n_lon, *refs):
    (
        obs_hbm, gau_hbm, back_hbm, spread_hbm, cols_hbm,
        r0_out, r1_out, r2_out, r3_out, q0_out, q1_out, q2_out, q3_out, first_out, second_out, mix_out,
        obs_ref, gau_ref, back, spread, table, obs_pad, obs_tile, gau_pad, gau_send, gau_recv, extended,
        up_send, down_send, from_up, from_down, swath_src, swath_dst, red_src, red_plane, red_line,
        load_sem, obs_sem, gau_sem, strip_sem, swath_sem, plane_sem, line_sem,
    ) = refs
    r_out = (r0_out, r1_out, r2_out, r3_out)
    q_out = (q0_out, q1_out, q2_out, q3_out)
    lat, lon = lax.axis_index("lat"), lax.axis_index("lon")
    rows, cols = gau_hbm.shape
    width = cols + 2 * HALO
    swath = obs_hbm.shape[0]
    lanes = [lanes_of(width, s) for s in SPACINGS]
    starts = [sum(lanes[:k]) for k in range(LEVELS)]
    heights = [rows // s + 2 * MARGIN for s in SPACINGS]
    tops = [sum(heights[:k]) for k in range(LEVELS)]

    def lon_peer(d):
        return lax.rem(lon + d, n_lon)

    def lat_peer(d):
        return lax.rem(lat + d, n_lat)

    def plane_peer(e):
        twin = lat + 1 - 2 * lax.rem(lat, 2)
        return {"lat": jnp.where(e >= n_lon, twin, lat), "lon": lon_peer(e)}

    def line_peer(f):
        return {"lat": lat_peer(2 * f)}

    barrier = pltpu.get_barrier_semaphore()

    def greet_line(f, c):
        pl.semaphore_signal(barrier, inc=1, device_id=line_peer(f), device_id_type=MESH)
        return c

    def greet_plane(e, c):
        pl.semaphore_signal(barrier, inc=1, device_id=plane_peer(e), device_id_type=MESH)
        return c

    beyond = {"lat": lax.rem(lat + n_lat - 1 + 2 * lax.rem(lat, 2), n_lat)}
    lax.fori_loop(1, n_lat // 2, greet_line, 0)
    pl.semaphore_signal(barrier, inc=1, device_id=beyond, device_id_type=MESH)
    lax.fori_loop(1, 2 * n_lon, greet_plane, 0)

    loads = [
        pltpu.make_async_copy(src, dst, load_sem.at[i])
        for i, (src, dst) in enumerate(
            ((obs_hbm, obs_ref), (gau_hbm, gau_ref), (back_hbm, back), (spread_hbm, spread), (cols_hbm, table))
        )
    ]
    for load in loads:
        load.start()
    extended[...] = jnp.zeros_like(extended)
    for load in loads:
        load.wait()
    obs_pad[:, :128] = jnp.zeros((swath, 128), F32)
    obs_pad[:, n_lon * cols :] = jnp.zeros((swath, 128), F32)
    obs_pad[:, HALO : HALO + n_lon * cols] = obs_ref[...]
    gau_pad[:, :128] = jnp.zeros((rows, 128), F32)
    gau_pad[:, cols:] = jnp.zeros((rows, 128), F32)
    gauge = gau_ref[...].astype(F32)
    gau_pad[:, HALO : HALO + cols] = gauge
    half = rows // 2
    lane = lax.broadcasted_iota(jnp.int32, (half, 128), 1)
    last, first = gauge[:, cols - 128 :], gauge[:, :128]
    gau_send[0] = jnp.where(lane < HALO, roll(last[:half], HALO, 1), last[half:])
    gau_send[1] = jnp.where(lane < HALO, first[:half], roll(first[half:], HALO, 1))

    pl.semaphore_wait(barrier, n_lat // 2 - 1 + 1 + 2 * n_lon - 1)

    def scatter(d, c):
        peer = lon_peer(d)
        pltpu.make_async_remote_copy(
            src_ref=obs_pad.at[:, pl.ds(pl.multiple_of(peer * cols, 128), width)],
            dst_ref=obs_tile.at[pl.ds(pl.multiple_of(lon * swath, 8), swath), :],
            send_sem=obs_sem.at[0],
            recv_sem=obs_sem.at[1],
            device_id={"lon": peer},
            device_id_type=MESH,
        ).start()
        return c

    def beside(which, d):
        return pltpu.make_async_remote_copy(
            src_ref=gau_send.at[which],
            dst_ref=gau_recv.at[which],
            send_sem=gau_sem.at[2 * which],
            recv_sem=gau_sem.at[2 * which + 1],
            device_id={"lon": lon_peer(d)},
            device_id_type=MESH,
        )

    to_right, to_left = beside(0, 1), beside(1, n_lon - 1)
    lax.fori_loop(1, n_lon, scatter, 0)
    to_right.start()
    to_left.start()
    own = pl.ds(pl.multiple_of(lon * swath, 8), swath)
    obs_tile[own, :] = obs_pad[:, pl.ds(pl.multiple_of(lon * cols, 128), width)]

    to_right.wait()
    to_left.wait()
    packed = gau_recv[0] * jnp.where(lon > 0, 1.0, 0.0)
    gau_pad[:half, :128] = jnp.where(lane < HALO, packed, gau_pad[:half, :128])
    gau_pad[half:, :128] = jnp.where(lane < HALO, roll(packed, HALO, 1), gau_pad[half:, :128])
    packed = gau_recv[1] * jnp.where(lon < n_lon - 1, 1.0, 0.0)
    gau_pad[:half, cols:] = jnp.where(lane < HALO, gau_pad[:half, cols:], roll(packed, HALO, 1))
    gau_pad[half:, cols:] = jnp.where(lane < HALO, gau_pad[half:, cols:], packed)
    all_obs = obs_tile.at[: (n_lon - 1) * swath]
    pltpu.make_async_copy(all_obs, all_obs, obs_sem.at[1]).wait()
    pltpu.make_async_copy(all_obs, all_obs, obs_sem.at[0]).wait()

    valid = []
    inside = []
    for k, s in enumerate(SPACINGS):
        row = lax.broadcasted_iota(jnp.int32, (heights[k], 1), 0) - MARGIN
        col = lax.broadcasted_iota(jnp.int32, (1, lanes[k]), 1) - HALO // s
        row_global, col_global = row + lat * (rows // s), col + lon * (cols // s)
        row_ok = jnp.where((row_global >= 0) & (row_global < n_lat * (rows // s)), 1.0, 0.0)
        col_ok = jnp.where((col_global >= 0) & (col_global < n_lon * (cols // s)), 1.0, 0.0)
        valid.append(row_ok * col_ok)
        inside.append(jnp.where((col >= 0) & (col < cols // s), 1.0, 0.0))

    def adjoint(misfit):
        part = into(back[...], misfit)
        result = []
        for k in range(3):
            at = slice(starts[k], starts[k] + lanes[k])
            result.append(times(part[tops[k] : tops[k] + heights[k]], table[:width, at], table[width:, at]))
        extended[MARGIN : MARGIN + rows, :] = five(misfit, 1)
        result.append(five(extended[...], 0))
        return result

    def forward(coeffs):
        parts = [into(spread[:, 128 * k : 128 * k + heights[k]], coeffs[k]) for k in range(3)]
        coarse = times(jnp.concatenate(parts, axis=1), table[:width], table[width:], transposed=True)
        fine = five(coeffs[3], 0)[MARGIN : MARGIN + rows]
        return coarse + five(fine, 1)

    def strips(which, partial):
        for k in range(LEVELS):
            at = slice(starts[k], starts[k] + lanes[k])
            up_send[which, :, at] = partial[k][:8]
            down_send[which, :, at] = partial[k][heights[k] - 8 :]
        copies = []
        for j, (src, dst, d) in enumerate(((up_send, from_down, n_lat - 1), (down_send, from_up, 1))):
            copies.append(
                pltpu.make_async_remote_copy(
                    src_ref=src.at[which],
                    dst_ref=dst.at[which],
                    send_sem=strip_sem.at[4 * which + 2 * j],
                    recv_sem=strip_sem.at[4 * which + 2 * j + 1],
                    device_id={"lat": lat_peer(d)},
                    device_id_type=MESH,
                )
            )
            copies[-1].start()
        return copies

    def joined(which, partial):
        result = []
        has_up = jnp.where(lat > 0, 1.0, 0.0)
        has_down = jnp.where(lat < n_lat - 1, 1.0, 0.0)
        for k in range(LEVELS):
            at = slice(starts[k], starts[k] + lanes[k])
            head = partial[k][:8] + has_up * from_up[which, :, at]
            tail = partial[k][heights[k] - 8 :] + has_down * from_down[which, :, at]
            middle = partial[k][8 : heights[k] - 8]
            result.append(jnp.concatenate([head, middle, tail], axis=0) * valid[k])
        return result

    def send_swaths(which):
        def push(d, c):
            peer = lon_peer(d)
            pltpu.make_async_remote_copy(
                src_ref=swath_src.at[which, pl.ds(pl.multiple_of(peer * swath, 8), swath), :],
                dst_ref=swath_dst.at[which, :, pl.ds(pl.multiple_of(lon * cols, 128), cols)],
                send_sem=swath_sem.at[2 * which],
                recv_sem=swath_sem.at[2 * which + 1],
                device_id={"lon": peer},
                device_id_type=MESH,
            ).start()
            return c

        lax.fori_loop(1, n_lon, push, 0)
        at = pl.ds(pl.multiple_of(lon * cols, 128), cols)
        swath_dst[which, :, at] = swath_src[which, own, :]

    def extract(k, x):
        s = SPACINGS[k]
        return x[MARGIN : MARGIN + rows // s, HALO // s : HALO // s + cols // s]

    above = lax.broadcasted_iota(jnp.int32, (8, 1), 0) >= MARGIN

    def squares(k, x):
        y = x * x
        n = heights[k]
        ends = jnp.where(above, y[:8], 0.0) + jnp.where(above, 0.0, y[n - 8 :])
        return fold_lanes((fold(y[8 : n - 8]) + ends) * inside[k])

    lane = lax.broadcasted_iota(jnp.int32, (1, width), 1)
    own_lane = jnp.where((lane >= HALO) & (lane < HALO + cols), 1.0, 0.0)

    def misfits(surface):
        misfit = 2.0 * gau_pad[...] * surface
        return misfit, fold_lanes(fold(misfit * surface) * own_lane)

    partial = adjoint(2.0 * gau_pad[...] * obs_tile[...])
    copies = strips(0, partial)
    for copy in copies:
        copy.wait()
    right = joined(0, partial)

    surface = forward(right)
    misfit, mu1 = misfits(surface)
    partial = adjoint(misfit)
    copies = strips(1, partial)
    swath_src[0] = surface[:, HALO : HALO + cols]
    send_swaths(0)
    mu0 = jnp.zeros((8, 128), F32)
    rough = []
    for k in range(LEVELS):
        smooth = stencil(right[k]) * valid[k]
        rough.append(SCALES[k] * stencil(smooth) * valid[k])
        mu0 = mu0 + squares(k, right[k])
        mu1 = mu1 + SCALES[k] * squares(k, smooth)
        r_out[k][...] = extract(k, right[k])
    for copy in copies:
        copy.wait()
    image = [x + y for x, y in zip(joined(1, partial), rough)]

    surface = forward(image)
    mu2 = jnp.zeros((8, 128), F32)
    _, mu3 = misfits(surface)
    for k in range(LEVELS):
        mu2 = mu2 + squares(k, image[k])
        mu3 = mu3 + SCALES[k] * squares(k, stencil(image[k]) * valid[k])

    row8 = lax.broadcasted_iota(jnp.int32, (8, 128), 0)
    lane8 = lax.broadcasted_iota(jnp.int32, (8, 128), 1)

    def reduce_start(stage, value, dst, sem, count, peer_of):
        red_src[stage] = value

        def push(d, c):
            pltpu.make_async_remote_copy(
                src_ref=red_src.at[stage],
                dst_ref=dst.at[d - 1],
                send_sem=sem.at[0],
                recv_sem=sem.at[1],
                device_id=peer_of(d),
                device_id_type=MESH,
            ).start()
            return c

        lax.fori_loop(1, count, push, 0)

    def reduce_end(value, dst, sem):
        pltpu.make_async_copy(dst, dst, sem.at[1]).wait()
        return value + jnp.sum(dst[...], axis=0)

    gathered = jnp.zeros((8, 128), F32)
    for i, value in enumerate((mu0, mu1, mu2, mu3)):
        gathered = gathered + jnp.where(row8 == i, jnp.sum(value, axis=0, keepdims=True), 0.0)
    gathered = jnp.sum(gathered, axis=1, keepdims=True)
    moments = jnp.sum(jnp.where(row8 == lane8, gathered, 0.0), axis=0, keepdims=True)
    reduce_start(0, moments, red_plane, plane_sem, 2 * n_lon, plane_peer)
    swath_src[1] = surface[:, HALO : HALO + cols]
    for k in range(LEVELS):
        q_out[k][...] = extract(k, image[k])
    moments = reduce_end(moments, red_plane, plane_sem)
    reduce_start(1, moments, red_line, line_sem, n_lat // 2, line_peer)
    send_swaths(1)
    moments = reduce_end(moments, red_line, line_sem)

    m0, m1, m2, m3 = (moments[:, i : i + 1] for i in range(4))
    alpha = m0 / m1
    grow = alpha * m2 / m1
    second_norm = alpha * alpha * m2 - m0
    curv = alpha * alpha * m3 - grow * grow * m1
    gamma = second_norm / curv
    lane1 = lane8[:1]
    mix_out[...] = jnp.where(lane1 == 0, alpha + gamma * grow, 0.0) + jnp.where(lane1 == 1, -alpha * gamma, 0.0)

    everything = swath_dst.at[0, :, : (n_lon - 1) * cols]
    for i in range(4):
        pltpu.make_async_copy(everything, everything, swath_sem.at[i]).wait()
    pltpu.make_async_copy(red_plane, red_plane, plane_sem.at[0]).wait()
    pltpu.make_async_copy(red_line, red_line, line_sem.at[0]).wait()
    first_out[...] = swath_dst[0]
    second_out[...] = swath_dst[1]


def combine(*refs):
    mix = refs[0][...]
    a, b = mix[:, 0:1], mix[:, 1:2]
    count = LEVELS + 1
    for first, second, out in zip(refs[1 : 1 + count], refs[1 + count : 1 + 2 * count], refs[1 + 2 * count :]):
        out[...] = a * first[...] + b * second[...]


def body(observed, gauged):
    n_lat, n_lon = lax.axis_size("lat"), lax.axis_size("lon")
    rows, cols = gauged.shape
    swath = observed.shape[0]
    width = cols + 2 * HALO
    back, spread, table = tables(rows, cols)
    level_shapes = [jax.ShapeDtypeStruct((rows // s, cols // s), F32) for s in SPACINGS]
    swath_shape = jax.ShapeDtypeStruct(observed.shape, F32)
    strip = 8 * sum(lanes_of(width, s) for s in SPACINGS)
    vmem = pl.BlockSpec(memory_space=pltpu.VMEM)
    anywhere = pl.BlockSpec(memory_space=pl.ANY)
    dma = pltpu.SemaphoreType.DMA
    *pieces, mix = pl.pallas_call(
        functools.partial(kernel, n_lat, n_lon),
        out_shape=[pltpu.VMEM(x.shape, F32) for x in (*level_shapes, *level_shapes, swath_shape, swath_shape)]
        + [pltpu.VMEM((1, 128), F32)],
        in_specs=[anywhere] * 5,
        out_specs=[vmem] * 11,
        scratch_shapes=[
            pltpu.VMEM(observed.shape, F32),
            pltpu.VMEM(gauged.shape, gauged.dtype),
            pltpu.VMEM(back.shape, BF16),
            pltpu.VMEM(spread.shape, BF16),
            pltpu.VMEM(table.shape, BF16),
            pltpu.VMEM((swath, n_lon * cols + 2 * HALO), F32),
            pltpu.VMEM((rows, width), F32),
            pltpu.VMEM((rows, width), F32),
            pltpu.VMEM((2, rows // 2, 128), F32),
            pltpu.VMEM((2, rows // 2, 128), F32),
            pltpu.VMEM((rows + 2 * MARGIN, width), F32),
            *[pltpu.VMEM((2, 8, strip // 8), F32)] * 4,
            pltpu.VMEM((2, rows, cols), F32),
            pltpu.VMEM((2, swath, n_lon * cols), F32),
            pltpu.VMEM((2, 1, 128), F32),
            pltpu.VMEM((2 * n_lon - 1, 1, 128), F32),
            pltpu.VMEM((n_lat // 2 - 1, 1, 128), F32),
            dma((5,)),
            dma((2,)),
            dma((4,)),
            dma((8,)),
            dma((4,)),
            dma((2,)),
            dma((2,)),
        ],
        compiler_params=pltpu.CompilerParams(collective_id=0, has_side_effects=True),
        name="krylov",
    )(observed, gauged, back, spread, table)
    mix, *pieces = [pltpu.with_memory_space_constraint(x, pltpu.VMEM) for x in (mix, *pieces)]
    firsts = [*pieces[:LEVELS], pieces[2 * LEVELS]]
    seconds = [*pieces[LEVELS : 2 * LEVELS], pieces[2 * LEVELS + 1]]
    return pl.pallas_call(
        combine,
        out_shape=(*level_shapes, swath_shape),
        in_specs=[vmem] * 11,
        out_specs=[vmem] * 5,
        name="combine",
    )(mix, *firsts, *seconds)


def solution(mesh):
    tile = P("lat", "lon")
    swaths = P(("lat", "lon"), None)
    return jax.shard_map(
        body,
        mesh=mesh,
        in_specs=(swaths, tile),
        out_specs=(tile, tile, tile, tile, swaths),
        check_vma=False,
    )
```

```python
import functools
import math

import jax
import jax.numpy as jnp
import numpy as np
from jax import lax
from jax.experimental import pallas as pl
from jax.experimental.pallas import tpu as pltpu
from jax.sharding import PartitionSpec as P

LEVELS = 4
SPACINGS = (8, 4, 2, 1)
SCALES = (0.02, 0.03, 0.05, 0.08)
HALO = 64
MARGIN = 4
MESH = pl.DeviceIdType.MESH
F32 = jnp.float32
BF16 = jnp.bfloat16


def weight(cells, nodes, spacing):
    numerator = np.abs(2 * cells - 2 * spacing * nodes - (spacing - 1))
    d = numerator / (5.0 * spacing)
    value = np.maximum(1.0 - d, 0.0) ** 6 * (35.0 * d * d + 18.0 * d + 3.0) / 3.0
    return value / math.sqrt(spacing)


def halves(table):
    table = np.asarray(table, np.float32)
    high = table.astype(BF16)
    low = (table - high.astype(np.float32)).astype(BF16)
    return jnp.asarray(np.concatenate([high, low], axis=0))


def lanes_of(width, spacing):
    return -(-(width // spacing) // 128) * 128


def tables(rows, cols):
    width = cols + 2 * HALO
    row_parts, col_parts = [], []
    for s in SPACINGS[:3]:
        nodes = np.arange(rows // s + 2 * MARGIN) - MARGIN
        row_parts.append(weight(np.arange(rows)[None, :], nodes[:, None], s))
        nodes = np.arange(width // s) - HALO // s
        part = np.zeros((width, lanes_of(width, s)))
        part[:, : width // s] = weight(np.arange(width)[:, None] - HALO, nodes[None, :], s)
        col_parts.append(part)
    back = np.concatenate(row_parts, axis=0)
    spread = np.zeros((rows, 128 * len(row_parts)))
    for k, part in enumerate(row_parts):
        spread[:, 128 * k : 128 * k + part.shape[0]] = part.T
    edges = [x for part in row_parts for x in (part[:8], part[-8:])]
    return halves(back), halves(np.concatenate(edges)), halves(spread), halves(np.concatenate(col_parts, axis=1))


def halve(x):
    high = x.astype(BF16).astype(F32)
    return jnp.concatenate([high, x - high], axis=0).astype(BF16)


def times(x, high, low, transposed=False):
    contract = (((1,), (1 if transposed else 0,)), ((), ()))
    n = x.shape[0]
    x = halve(x)
    both = lax.dot_general(x, high, contract, preferred_element_type=F32)
    rest = lax.dot_general(x[:n], low, contract, preferred_element_type=F32)
    return both[:n] + both[n:] + rest


def into(table, x):
    n = table.shape[0] // 2
    high = x.astype(BF16)
    low = (x - high.astype(F32)).astype(BF16)
    both = jnp.dot(table, high, preferred_element_type=F32)
    rest = jnp.dot(table[:n], low, preferred_element_type=F32)
    return both[:n] + both[n:] + rest


def roll(x, shift, axis):
    return pltpu.roll(x, shift % x.shape[axis], axis)


TAPS = [float(np.float32(weight(np.int64(0), np.int64(o), 1))) for o in range(3)]


def five(x, axis):
    near = roll(x, 1, axis) + roll(x, -1, axis)
    far = roll(x, 2, axis) + roll(x, -2, axis)
    return TAPS[0] * x + TAPS[1] * near + TAPS[2] * far


def stencil(x):
    return 5.0 * x - (roll(x, 1, 0) + roll(x, -1, 0) + roll(x, 1, 1) + roll(x, -1, 1))


def fold(x):
    return jnp.sum(x.reshape(x.shape[0] // 8, 8, x.shape[1]), axis=0)


def fold_lanes(x):
    result = x[:, :128]
    for at in range(128, x.shape[1], 128):
        result = result + x[:, at : at + 128]
    return result


def kernel(n_lat, n_lon, *refs):
    (
        obs_hbm, gau_hbm, back_hbm, edge_hbm, spread_hbm, cols_hbm,
        r0_out, r1_out, r2_out, r3_out, q0_out, q1_out, q2_out, q3_out, first_out, second_out, mix_out,
        obs_ref, gau_ref, back, edge, spread, table, obs_pad, obs_tile, gau_pad, gau_send, gau_recv, extended,
        part0, part1, part2, part3, right0, right1, right2, right3, surface_ref, mu_ref, strip_send, strip_recv, swath_src, swath_dst, red_src, red_plane, red_line,
        load_sem, obs_sem, gau_sem, strip_sem, swath_sem, plane_sem, line_sem, line_ready,
    ) = refs
    part_ref = (part0, part1, part2, part3)
    right_ref = (right0, right1, right2, right3)
    r_out = (r0_out, r1_out, r2_out, r3_out)
    q_out = (q0_out, q1_out, q2_out, q3_out)
    lat, lon = lax.axis_index("lat"), lax.axis_index("lon")
    rows, cols = gau_hbm.shape
    width = cols + 2 * HALO
    swath = obs_hbm.shape[0]
    lanes = [lanes_of(width, s) for s in SPACINGS]
    starts = [sum(lanes[:k]) for k in range(LEVELS)]
    heights = [rows // s + 2 * MARGIN for s in SPACINGS]
    tops = [sum(heights[:k]) for k in range(LEVELS)]

    def lon_peer(d):
        return lax.rem(lon + d, n_lon)

    def lat_peer(d):
        return lax.rem(lat + d, n_lat)

    twin = lat + 1 - 2 * lax.rem(lat, 2)

    def plane_peer(e):
        return {"lat": twin if e >= n_lon else lat, "lon": lon_peer(e)}

    def line_peer(f):
        return {"lat": lat_peer(2 * f)}

    loads = [
        pltpu.make_async_copy(src, dst, load_sem.at[i])
        for i, (src, dst) in enumerate(
            (
                (obs_hbm, obs_ref),
                (gau_hbm, gau_ref),
                (edge_hbm, edge),
                (cols_hbm, table),
                (back_hbm, back),
                (spread_hbm, spread),
            )
        )
    ]
    for load in loads:
        load.start()

    valid = []
    inside = []
    for k, s in enumerate(SPACINGS):
        row = lax.broadcasted_iota(jnp.int32, (heights[k], 1), 0) - MARGIN
        col = lax.broadcasted_iota(jnp.int32, (1, lanes[k]), 1) - HALO // s
        row_global, col_global = row + lat * (rows // s), col + lon * (cols // s)
        row_ok = jnp.where((row_global >= 0) & (row_global < n_lat * (rows // s)), 1.0, 0.0)
        col_ok = jnp.where((col_global >= 0) & (col_global < n_lon * (cols // s)), 1.0, 0.0)
        valid.append(row_ok * col_ok)
        inside.append(jnp.where((col >= 0) & (col < cols // s), 1.0, 0.0))

    barrier = pltpu.get_barrier_semaphore()
    beyond = {"lat": lax.rem(lat + n_lat - 1 + 2 * lax.rem(lat, 2), n_lat)}
    planes = n_lat // 2
    line = sorted(range(1, planes), key=lambda f: abs(f - planes // 2))
    reach = max(planes // 4, 1)
    near = [f for f in line if min(f, planes - f) <= reach]
    plane = sorted(range(1, 2 * n_lon), key=lambda e: abs(e % n_lon - n_lon // 2))
    for f in near:
        pl.semaphore_signal(barrier, inc=1, device_id=line_peer(f), device_id_type=MESH)
    for e in plane:
        pl.semaphore_signal(barrier, inc=1, device_id=plane_peer(e), device_id_type=MESH)
    pl.semaphore_signal(barrier, inc=1, device_id=beyond, device_id_type=MESH)

    extended[...] = jnp.zeros_like(extended)
    loads[0].wait()
    loads[1].wait()
    obs_pad[:, :128] = jnp.zeros((swath, 128), F32)
    obs_pad[:, n_lon * cols :] = jnp.zeros((swath, 128), F32)
    obs_pad[:, HALO : HALO + n_lon * cols] = obs_ref[...]
    gau_pad[:, :128] = jnp.zeros((rows, 128), F32)
    gau_pad[:, cols:] = jnp.zeros((rows, 128), F32)
    gauge = gau_ref[...].astype(F32)
    gau_pad[:, HALO : HALO + cols] = gauge
    half = rows // 2
    lane = lax.broadcasted_iota(jnp.int32, (half, 128), 1)
    last, first = gauge[:, cols - 128 :], gauge[:, :128]
    gau_send[0] = jnp.where(lane < HALO, roll(last[:half], HALO, 1), last[half:])
    gau_send[1] = jnp.where(lane < HALO, first[:half], roll(first[half:], HALO, 1))

    pl.semaphore_wait(barrier, len(near) + 1 + 2 * n_lon - 1)
    for f in (reach, planes - reach):
        pl.semaphore_signal(line_ready, inc=1, device_id=line_peer(f), device_id_type=MESH)

    def scatter(d, c):
        peer = lon_peer(d)
        pltpu.make_async_remote_copy(
            src_ref=obs_pad.at[:, pl.ds(pl.multiple_of(peer * cols, 128), width)],
            dst_ref=obs_tile.at[pl.ds(pl.multiple_of(lon * swath, 8), swath), :],
            send_sem=obs_sem.at[0],
            recv_sem=obs_sem.at[1],
            device_id={"lon": peer},
            device_id_type=MESH,
        ).start()
        return c

    def beside(which, d):
        return pltpu.make_async_remote_copy(
            src_ref=gau_send.at[which],
            dst_ref=gau_recv.at[which],
            send_sem=gau_sem.at[2 * which],
            recv_sem=gau_sem.at[2 * which + 1],
            device_id={"lon": lon_peer(d)},
            device_id_type=MESH,
        )

    to_right, to_left = beside(0, 1), beside(1, n_lon - 1)
    lax.fori_loop(1, n_lon, scatter, 0)
    to_right.start()
    to_left.start()
    own = pl.ds(pl.multiple_of(lon * swath, 8), swath)
    obs_tile[own, :] = obs_pad[:, pl.ds(pl.multiple_of(lon * cols, 128), width)]

    for load in loads[2:]:
        load.wait()
    to_right.wait()
    to_left.wait()
    packed = gau_recv[0] * jnp.where(lon > 0, 1.0, 0.0)
    gau_pad[:half, :128] = jnp.where(lane < HALO, packed, gau_pad[:half, :128])
    gau_pad[half:, :128] = jnp.where(lane < HALO, roll(packed, HALO, 1), gau_pad[half:, :128])
    packed = gau_recv[1] * jnp.where(lon < n_lon - 1, 1.0, 0.0)
    gau_pad[:half, cols:] = jnp.where(lane < HALO, gau_pad[:half, cols:], roll(packed, HALO, 1))
    gau_pad[half:, cols:] = jnp.where(lane < HALO, gau_pad[half:, cols:], packed)
    all_obs = obs_tile.at[: (n_lon - 1) * swath]
    pltpu.make_async_copy(all_obs, all_obs, obs_sem.at[1]).wait()
    pltpu.make_async_copy(all_obs, all_obs, obs_sem.at[0]).wait()

    row8 = lax.broadcasted_iota(jnp.int32, (8, 1), 0)
    above = row8 >= MARGIN
    summed = (row8 >= 2) & (row8 < 6)

    def span(k):
        return slice(starts[k], starts[k] + lanes[k])

    def adjoint(misfit):
        part = into(back[...], misfit)
        for k in range(3):
            rows_k = part[tops[k] : tops[k] + heights[k]]
            part_ref[k][...] = times(rows_k, table[:width, span(k)], table[width:, span(k)])
        extended[MARGIN : MARGIN + rows, :] = five(misfit, 1)
        part3[...] = five(extended[...], 0)

    def adjoint_edges(misfit):
        part = into(edge[...], misfit)
        heads, tails = [], []
        for k in range(3):
            both = times(part[16 * k : 16 * k + 16], table[:width, span(k)], table[width:, span(k)])
            heads.append(both[:8])
            tails.append(both[8:])
        near, away = five(misfit[:8], 1), five(misfit[rows - 8 :], 1)
        heads.append(five(jnp.where(above, roll(near, 4, 0), 0.0), 0))
        tails.append(five(jnp.where(above, 0.0, roll(away, 4, 0)), 0))
        return heads, tails

    def forward(coeffs):
        parts = [into(spread[:, 128 * k : 128 * k + heights[k]], coeffs[k]) for k in range(3)]
        coarse = times(jnp.concatenate(parts, axis=1), table[:width], table[width:], transposed=True)
        fine = five(coeffs[3], 0)[MARGIN : MARGIN + rows]
        return coarse + five(fine, 1)

    def strips(which, heads, tails):
        copies = []
        for j, (tile, d) in enumerate(((heads, n_lat - 1), (tails, 1))):
            coarse = roll(jnp.concatenate(tile[:3], axis=1), 2, 0)
            fine = roll(tile[3], -2, 0)
            strip_send[which, j, :, :width] = jnp.where(above, coarse[:, :width], fine)
            strip_send[which, j, :, width:] = coarse[:, width:]
            copies.append(
                pltpu.make_async_remote_copy(
                    src_ref=strip_send.at[which, j],
                    dst_ref=strip_recv.at[which, j],
                    send_sem=strip_sem.at[4 * which + 2 * j],
                    recv_sem=strip_sem.at[4 * which + 2 * j + 1],
                    device_id={"lat": lat_peer(d)},
                    device_id_type=MESH,
                )
            )
            copies[-1].start()
        return copies

    def received(which, j, has):
        packed = strip_recv[which, j] * has
        coarse = jnp.where(summed, roll(packed, -2, 0), 0.0)
        fine = jnp.where(summed, roll(packed[:, :width], 2, 0), 0.0)
        return [coarse[:, span(k)] for k in range(3)] + [fine]

    def joined(which, extra=None):
        above_it = received(which, 1, jnp.where(lat > 0, 1.0, 0.0))
        below_it = received(which, 0, jnp.where(lat < n_lat - 1, 1.0, 0.0))
        result = []
        for k in range(LEVELS):
            partial = part_ref[k][...]
            if extra:
                partial = partial + extra[k]
            head = partial[:8] + above_it[k]
            tail = partial[heights[k] - 8 :] + below_it[k]
            middle = partial[8 : heights[k] - 8]
            result.append(jnp.concatenate([head, middle, tail], axis=0) * valid[k])
        return result

    def send_swaths(which):
        def push(d, c):
            peer = lon_peer(d)
            pltpu.make_async_remote_copy(
                src_ref=swath_src.at[which, pl.ds(pl.multiple_of(peer * swath, 8), swath), :],
                dst_ref=swath_dst.at[which, :, pl.ds(pl.multiple_of(lon * cols, 128), cols)],
                send_sem=swath_sem.at[2 * which],
                recv_sem=swath_sem.at[2 * which + 1],
                device_id={"lon": peer},
                device_id_type=MESH,
            ).start()
            return c

        lax.fori_loop(1, n_lon, push, 0)
        at = pl.ds(pl.multiple_of(lon * cols, 128), cols)
        swath_dst[which, :, at] = swath_src[which, own, :]

    def extract(k, x):
        s = SPACINGS[k]
        return x[MARGIN : MARGIN + rows // s, HALO // s : HALO // s + cols // s]


    def squares(k, x):
        y = x * x
        n = heights[k]
        ends = jnp.where(above, y[:8], 0.0) + jnp.where(above, 0.0, y[n - 8 :])
        return fold_lanes((fold(y[8 : n - 8]) + ends) * inside[k])

    lane = lax.broadcasted_iota(jnp.int32, (1, width), 1)
    own_lane = jnp.where((lane >= HALO) & (lane < HALO + cols), 1.0, 0.0)

    def misfits(surface):
        misfit = 2.0 * gau_pad[...] * surface
        return misfit, fold_lanes(fold(misfit * surface) * own_lane)

    misfit = 2.0 * gau_pad[...] * obs_tile[...]
    copies = strips(0, *adjoint_edges(misfit))

    @pl.when(lat >= 0)
    def _():
        adjoint(2.0 * gau_pad[...] * obs_tile[...])

    for copy in copies:
        copy.wait()
    right = joined(0)

    surface = forward(right)
    surface_ref[...] = surface
    heads, tails = adjoint_edges(2.0 * gau_pad[...] * surface)
    for k in range(LEVELS):
        n = heights[k]
        for tile, x, ok, own_rows in (
            (heads, right[k][:8], valid[k][:8], above),
            (tails, right[k][n - 8 :], valid[k][n - 8 :], ~above),
        ):
            tile[k] = tile[k] + SCALES[k] * stencil(stencil(jnp.where(own_rows, x, 0.0)) * ok)
    copies = strips(1, heads, tails)
    for k in range(LEVELS):
        right_ref[k][...] = right[k]

    @pl.when(lat >= 0)
    def _():
        misfit, mu1 = misfits(surface_ref[...])
        adjoint(misfit)
        mu0 = jnp.zeros((8, 128), F32)
        for k in range(LEVELS):
            x = right_ref[k][...]
            n = heights[k]
            head, tail = jnp.where(above, x[:8], 0.0), jnp.where(above, 0.0, x[n - 8 :])
            own_x = jnp.concatenate([head, x[8 : n - 8], tail], axis=0)
            part_ref[k][...] += SCALES[k] * stencil(stencil(own_x) * valid[k])
            mu0 = mu0 + squares(k, x)
            mu1 = mu1 + SCALES[k] * squares(k, stencil(x) * valid[k])
        mu_ref[0] = mu0
        mu_ref[1] = mu1

    for copy in copies:
        copy.wait()
    image = joined(1)

    surface = forward(image)
    mu2 = jnp.zeros((8, 128), F32)
    _, mu3 = misfits(surface)
    for k in range(LEVELS):
        mu2 = mu2 + squares(k, image[k])
        mu3 = mu3 + SCALES[k] * squares(k, stencil(image[k]) * valid[k])

    sub8 = lax.broadcasted_iota(jnp.int32, (8, 128), 0)
    lane8 = lax.broadcasted_iota(jnp.int32, (8, 128), 1)

    def reduce_start(stage, value, dst, sem, order, peer_of):
        red_src[stage] = value
        for d in order:
            pltpu.make_async_remote_copy(
                src_ref=red_src.at[stage],
                dst_ref=dst.at[d - 1],
                send_sem=sem.at[0],
                recv_sem=sem.at[1],
                device_id=peer_of(d),
                device_id_type=MESH,
            ).start()

    def reduce_end(value, dst, sem):
        pltpu.make_async_copy(dst, dst, sem.at[1]).wait()
        return value + jnp.sum(dst[...], axis=0)

    gathered = jnp.zeros((8, 128), F32)
    for i, value in enumerate((mu_ref[0], mu_ref[1], mu2, mu3)):
        gathered = gathered + jnp.where(sub8 == i, jnp.sum(value, axis=0, keepdims=True), 0.0)
    gathered = jnp.sum(gathered, axis=1, keepdims=True)
    moments = jnp.sum(jnp.where(sub8 == lane8, gathered, 0.0), axis=0, keepdims=True)
    reduce_start(0, moments, red_plane, plane_sem, plane, plane_peer)
    swath_src[0] = surface_ref[:, HALO : HALO + cols]
    send_swaths(0)
    swath_src[1] = surface[:, HALO : HALO + cols]
    for k in range(LEVELS):
        r_out[k][...] = extract(k, right_ref[k][...])
        q_out[k][...] = extract(k, image[k])
    moments = reduce_end(moments, red_plane, plane_sem)
    pl.semaphore_wait(line_ready, 2)
    reduce_start(1, moments, red_line, line_sem, line, line_peer)
    send_swaths(1)
    everything = swath_dst.at[0, :, : (n_lon - 1) * cols]
    for which, out in ((0, first_out), (1, second_out)):
        pltpu.make_async_copy(everything, everything, swath_sem.at[2 * which + 1]).wait()
        out[...] = swath_dst[which]
    moments = reduce_end(moments, red_line, line_sem)

    m0, m1, m2, m3 = (moments[:, i : i + 1] for i in range(4))
    alpha = m0 / m1
    grow = alpha * m2 / m1
    second_norm = alpha * alpha * m2 - m0
    curv = alpha * alpha * m3 - grow * grow * m1
    gamma = second_norm / curv
    lane1 = lane8[:1]
    mix_out[...] = jnp.where(lane1 == 0, alpha + gamma * grow, 0.0) + jnp.where(lane1 == 1, -alpha * gamma, 0.0)

    for which in range(2):
        pltpu.make_async_copy(everything, everything, swath_sem.at[2 * which]).wait()
    pltpu.make_async_copy(red_plane, red_plane, plane_sem.at[0]).wait()
    pltpu.make_async_copy(red_line, red_line, line_sem.at[0]).wait()


def combine(*refs):
    mix = refs[0][...]
    a, b = mix[:, 0:1], mix[:, 1:2]
    count = LEVELS + 1
    for first, second, out in zip(refs[1 : 1 + count], refs[1 + count : 1 + 2 * count], refs[1 + 2 * count :]):
        out[...] = a * first[...] + b * second[...]


def body(observed, gauged):
    n_lat, n_lon = lax.axis_size("lat"), lax.axis_size("lon")
    rows, cols = gauged.shape
    swath = observed.shape[0]
    width = cols + 2 * HALO
    back, edge, spread, table = tables(rows, cols)
    level_shapes = [jax.ShapeDtypeStruct((rows // s, cols // s), F32) for s in SPACINGS]
    swath_shape = jax.ShapeDtypeStruct(observed.shape, F32)
    node_shapes = [pltpu.VMEM((rows // s + 2 * MARGIN, lanes_of(width, s)), F32) for s in SPACINGS]
    vmem = pl.BlockSpec(memory_space=pltpu.VMEM)
    anywhere = pl.BlockSpec(memory_space=pl.ANY)
    dma = pltpu.SemaphoreType.DMA
    *pieces, mix = pl.pallas_call(
        functools.partial(kernel, n_lat, n_lon),
        out_shape=[pltpu.VMEM(x.shape, F32) for x in (*level_shapes, *level_shapes, swath_shape, swath_shape)]
        + [pltpu.VMEM((1, 128), F32)],
        in_specs=[anywhere] * 6,
        out_specs=[vmem] * 11,
        scratch_shapes=[
            pltpu.VMEM(observed.shape, F32),
            pltpu.VMEM(gauged.shape, gauged.dtype),
            pltpu.VMEM(back.shape, BF16),
            pltpu.VMEM(edge.shape, BF16),
            pltpu.VMEM(spread.shape, BF16),
            pltpu.VMEM(table.shape, BF16),
            pltpu.VMEM((swath, n_lon * cols + 2 * HALO), F32),
            pltpu.VMEM((rows, width), F32),
            pltpu.VMEM((rows, width), F32),
            pltpu.VMEM((2, rows // 2, 128), F32),
            pltpu.VMEM((2, rows // 2, 128), F32),
            pltpu.VMEM((rows + 2 * MARGIN, width), F32),
            *node_shapes,
            *node_shapes,
            pltpu.VMEM((rows, width), F32),
            pltpu.VMEM((2, 8, 128), F32),
            *[pltpu.VMEM((2, 2, 8, sum(lanes_of(width, s) for s in SPACINGS[:3])), F32)] * 2,
            pltpu.VMEM((2, rows, cols), F32),
            pltpu.VMEM((2, swath, n_lon * cols), F32),
            pltpu.VMEM((2, 1, 128), F32),
            pltpu.VMEM((2 * n_lon - 1, 1, 128), F32),
            pltpu.VMEM((n_lat // 2 - 1, 1, 128), F32),
            dma((6,)),
            dma((2,)),
            dma((4,)),
            dma((8,)),
            dma((4,)),
            dma((2,)),
            dma((2,)),
            pltpu.SemaphoreType.REGULAR,
        ],
        compiler_params=pltpu.CompilerParams(collective_id=0, has_side_effects=True),
        name="krylov",
    )(observed, gauged, back, edge, spread, table)
    mix, *pieces = [pltpu.with_memory_space_constraint(x, pltpu.VMEM) for x in (mix, *pieces)]
    firsts = [*pieces[:LEVELS], pieces[2 * LEVELS]]
    seconds = [*pieces[LEVELS : 2 * LEVELS], pieces[2 * LEVELS + 1]]
    return pl.pallas_call(
        combine,
        out_shape=(*level_shapes, swath_shape),
        in_specs=[vmem] * 11,
        out_specs=[vmem] * 5,
        name="combine",
    )(mix, *firsts, *seconds)


def solution(mesh):
    tile = P("lat", "lon")
    swaths = P(("lat", "lon"), None)
    return jax.shard_map(
        body,
        mesh=mesh,
        in_specs=(swaths, tile),
        out_specs=(tile, tile, tile, tile, swaths),
        check_vma=False,
    )
```

```python
import functools
import math

import jax
import jax.numpy as jnp
import numpy as np
from jax import lax
from jax.experimental import pallas as pl
from jax.experimental.pallas import tpu as pltpu
from jax.sharding import PartitionSpec as P

LEVELS = 4
SPACINGS = (8, 4, 2, 1)
SCALES = (0.02, 0.03, 0.05, 0.08)
HALO = 64
MARGIN = 4
MESH = pl.DeviceIdType.MESH
F32 = jnp.float32
BF16 = jnp.bfloat16


def weight(cells, nodes, spacing):
    numerator = np.abs(2 * cells - 2 * spacing * nodes - (spacing - 1))
    d = numerator / (5.0 * spacing)
    value = np.maximum(1.0 - d, 0.0) ** 6 * (35.0 * d * d + 18.0 * d + 3.0) / 3.0
    return value / math.sqrt(spacing)


def halves(table):
    table = np.asarray(table, np.float32)
    high = table.astype(BF16)
    low = (table - high.astype(np.float32)).astype(BF16)
    return jnp.asarray(np.concatenate([high, low], axis=0))


def lanes_of(width, spacing):
    return -(-(width // spacing) // 128) * 128


def tables(rows, cols):
    width = cols + 2 * HALO
    row_parts, col_parts = [], []
    for s in SPACINGS[:3]:
        nodes = np.arange(rows // s + 2 * MARGIN) - MARGIN
        row_parts.append(weight(np.arange(rows)[None, :], nodes[:, None], s))
        nodes = np.arange(width // s) - HALO // s
        part = np.zeros((width, lanes_of(width, s)))
        part[:, : width // s] = weight(np.arange(width)[:, None] - HALO, nodes[None, :], s)
        col_parts.append(part)
    back = np.concatenate(row_parts, axis=0)
    spread = np.zeros((rows, 128 * len(row_parts)))
    for k, part in enumerate(row_parts):
        spread[:, 128 * k : 128 * k + part.shape[0]] = part.T
    edges = [x for part in row_parts for x in (part[:8], part[-8:])]
    return halves(back), halves(np.concatenate(edges)), halves(spread), halves(np.concatenate(col_parts, axis=1))


def halve(x):
    high = x.astype(BF16).astype(F32)
    return jnp.concatenate([high, x - high], axis=0).astype(BF16)


def times(x, high, low, transposed=False):
    contract = (((1,), (1 if transposed else 0,)), ((), ()))
    n = x.shape[0]
    x = halve(x)
    both = lax.dot_general(x, high, contract, preferred_element_type=F32)
    rest = lax.dot_general(x[:n], low, contract, preferred_element_type=F32)
    return both[:n] + both[n:] + rest


def into(table, x):
    n = table.shape[0] // 2
    high = x.astype(BF16)
    low = (x - high.astype(F32)).astype(BF16)
    both = jnp.dot(table, high, preferred_element_type=F32)
    rest = jnp.dot(table[:n], low, preferred_element_type=F32)
    return both[:n] + both[n:] + rest


def roll(x, shift, axis):
    return pltpu.roll(x, shift % x.shape[axis], axis)


TAPS = [float(np.float32(weight(np.int64(0), np.int64(o), 1))) for o in range(3)]


def five(x, axis):
    near = roll(x, 1, axis) + roll(x, -1, axis)
    far = roll(x, 2, axis) + roll(x, -2, axis)
    return TAPS[0] * x + TAPS[1] * near + TAPS[2] * far


def stencil(x):
    return 5.0 * x - (roll(x, 1, 0) + roll(x, -1, 0) + roll(x, 1, 1) + roll(x, -1, 1))


def fold(x):
    return jnp.sum(x.reshape(x.shape[0] // 8, 8, x.shape[1]), axis=0)


def fold_lanes(x):
    result = x[:, :128]
    for at in range(128, x.shape[1], 128):
        result = result + x[:, at : at + 128]
    return result


def kernel(n_lat, n_lon, *refs):
    (
        obs_hbm, gau_hbm, back_hbm, edge_hbm, spread_hbm, cols_hbm,
        r0_out, r1_out, r2_out, r3_out, q0_out, q1_out, q2_out, q3_out, first_out, second_out, mix_out,
        obs_ref, gau_ref, back, edge, spread, table, obs_pad, obs_tile, gau_pad, gau_send, gau_recv, extended,
        part0, part1, part2, part3, right0, right1, right2, right3, surface_ref, mu_ref, strip_send, strip_recv, swath_src, swath_dst, red_src, red_plane, red_line,
        load_sem, obs_sem, gau_sem, strip_sem, swath_sem, plane_sem, line_sem, line_ready,
    ) = refs
    part_ref = (part0, part1, part2, part3)
    right_ref = (right0, right1, right2, right3)
    r_out = (r0_out, r1_out, r2_out, r3_out)
    q_out = (q0_out, q1_out, q2_out, q3_out)
    lat, lon = lax.axis_index("lat"), lax.axis_index("lon")
    rows, cols = gau_hbm.shape
    width = cols + 2 * HALO
    swath = obs_hbm.shape[0]
    lanes = [lanes_of(width, s) for s in SPACINGS]
    starts = [sum(lanes[:k]) for k in range(LEVELS)]
    heights = [rows // s + 2 * MARGIN for s in SPACINGS]
    tops = [sum(heights[:k]) for k in range(LEVELS)]

    def lon_peer(d):
        return lax.rem(lon + d, n_lon)

    def lon_partner(e):
        peer = lon
        for b in (1, 2, 4, 8):
            if e & b and b < n_lon:
                peer = peer + b - 2 * b * lax.rem(lon // b, 2)
        return peer

    order = sorted(range(1, n_lon), key=lambda e: (-(e & 2), -(e & 12), e & 1))

    def lat_peer(d):
        return lax.rem(lat + d, n_lat)

    twin = lat + 1 - 2 * lax.rem(lat, 2)

    def plane_peer(e):
        return {"lat": twin if e >= n_lon else lat, "lon": lon_peer(e)}

    def line_peer(f):
        return {"lat": lat_peer(2 * f)}

    loads = [
        pltpu.make_async_copy(src, dst, load_sem.at[i])
        for i, (src, dst) in enumerate(
            (
                (obs_hbm, obs_ref),
                (gau_hbm, gau_ref),
                (edge_hbm, edge),
                (cols_hbm, table),
                (back_hbm, back),
                (spread_hbm, spread),
            )
        )
    ]
    for load in loads:
        load.start()

    valid = []
    inside = []
    for k, s in enumerate(SPACINGS):
        row = lax.broadcasted_iota(jnp.int32, (heights[k], 1), 0) - MARGIN
        col = lax.broadcasted_iota(jnp.int32, (1, lanes[k]), 1) - HALO // s
        row_global, col_global = row + lat * (rows // s), col + lon * (cols // s)
        row_ok = jnp.where((row_global >= 0) & (row_global < n_lat * (rows // s)), 1.0, 0.0)
        col_ok = jnp.where((col_global >= 0) & (col_global < n_lon * (cols // s)), 1.0, 0.0)
        valid.append(row_ok * col_ok)
        inside.append(jnp.where((col >= 0) & (col < cols // s), 1.0, 0.0))

    barrier = pltpu.get_barrier_semaphore()
    beyond = {"lat": lax.rem(lat + n_lat - 1 + 2 * lax.rem(lat, 2), n_lat)}
    planes = n_lat // 2
    line = sorted(range(1, planes), key=lambda f: abs(f - planes // 2))
    reach = max(planes // 4, 1)
    near = [f for f in line if min(f, planes - f) <= reach]
    plane = sorted(range(1, 2 * n_lon), key=lambda e: abs(e % n_lon - n_lon // 2))
    for f in near:
        pl.semaphore_signal(barrier, inc=1, device_id=line_peer(f), device_id_type=MESH)
    for e in plane:
        pl.semaphore_signal(barrier, inc=1, device_id=plane_peer(e), device_id_type=MESH)
    pl.semaphore_signal(barrier, inc=1, device_id=beyond, device_id_type=MESH)

    extended[...] = jnp.zeros_like(extended)
    loads[0].wait()
    loads[1].wait()
    obs_pad[:, :128] = jnp.zeros((swath, 128), F32)
    obs_pad[:, n_lon * cols :] = jnp.zeros((swath, 128), F32)
    obs_pad[:, HALO : HALO + n_lon * cols] = obs_ref[...]
    gau_pad[:, :128] = jnp.zeros((rows, 128), F32)
    gau_pad[:, cols:] = jnp.zeros((rows, 128), F32)
    gauge = gau_ref[...].astype(F32)
    gau_pad[:, HALO : HALO + cols] = gauge
    half = rows // 2
    lane = lax.broadcasted_iota(jnp.int32, (half, 128), 1)
    last, first = gauge[:, cols - 128 :], gauge[:, :128]
    gau_send[0] = jnp.where(lane < HALO, roll(last[:half], HALO, 1), last[half:])
    gau_send[1] = jnp.where(lane < HALO, first[:half], roll(first[half:], HALO, 1))

    pl.semaphore_wait(barrier, len(near) + 1 + 2 * n_lon - 1)
    for f in (reach, planes - reach):
        pl.semaphore_signal(line_ready, inc=1, device_id=line_peer(f), device_id_type=MESH)

    def scatter(e):
        peer = lon_partner(e)
        pltpu.make_async_remote_copy(
            src_ref=obs_pad.at[:, pl.ds(pl.multiple_of(peer * cols, 128), width)],
            dst_ref=obs_tile.at[pl.ds(pl.multiple_of(lon * swath, 8), swath), :],
            send_sem=obs_sem.at[0],
            recv_sem=obs_sem.at[1],
            device_id={"lon": peer},
            device_id_type=MESH,
        ).start()

    def beside(which, d):
        return pltpu.make_async_remote_copy(
            src_ref=gau_send.at[which],
            dst_ref=gau_recv.at[which],
            send_sem=gau_sem.at[2 * which],
            recv_sem=gau_sem.at[2 * which + 1],
            device_id={"lon": lon_peer(d)},
            device_id_type=MESH,
        )

    to_right, to_left = beside(0, 1), beside(1, n_lon - 1)
    for e in order:
        scatter(e)
    to_right.start()
    to_left.start()
    own = pl.ds(pl.multiple_of(lon * swath, 8), swath)
    obs_tile[own, :] = obs_pad[:, pl.ds(pl.multiple_of(lon * cols, 128), width)]

    for load in loads[2:]:
        load.wait()
    to_right.wait()
    to_left.wait()
    packed = gau_recv[0] * jnp.where(lon > 0, 1.0, 0.0)
    gau_pad[:half, :128] = jnp.where(lane < HALO, packed, gau_pad[:half, :128])
    gau_pad[half:, :128] = jnp.where(lane < HALO, roll(packed, HALO, 1), gau_pad[half:, :128])
    packed = gau_recv[1] * jnp.where(lon < n_lon - 1, 1.0, 0.0)
    gau_pad[:half, cols:] = jnp.where(lane < HALO, gau_pad[:half, cols:], roll(packed, HALO, 1))
    gau_pad[half:, cols:] = jnp.where(lane < HALO, gau_pad[half:, cols:], packed)
    all_obs = obs_tile.at[: (n_lon - 1) * swath]
    pltpu.make_async_copy(all_obs, all_obs, obs_sem.at[1]).wait()
    pltpu.make_async_copy(all_obs, all_obs, obs_sem.at[0]).wait()

    row8 = lax.broadcasted_iota(jnp.int32, (8, 1), 0)
    above = row8 >= MARGIN
    summed = (row8 >= 2) & (row8 < 6)

    def span(k):
        return slice(starts[k], starts[k] + lanes[k])

    def adjoint(misfit):
        part = into(back[...], misfit)
        for k in range(3):
            rows_k = part[tops[k] : tops[k] + heights[k]]
            part_ref[k][...] = times(rows_k, table[:width, span(k)], table[width:, span(k)])
        extended[MARGIN : MARGIN + rows, :] = five(misfit, 1)
        part3[...] = five(extended[...], 0)

    def adjoint_edges(misfit):
        part = into(edge[...], misfit)
        heads, tails = [], []
        for k in range(3):
            both = times(part[16 * k : 16 * k + 16], table[:width, span(k)], table[width:, span(k)])
            heads.append(both[:8])
            tails.append(both[8:])
        near, away = five(misfit[:8], 1), five(misfit[rows - 8 :], 1)
        heads.append(five(jnp.where(above, roll(near, 4, 0), 0.0), 0))
        tails.append(five(jnp.where(above, 0.0, roll(away, 4, 0)), 0))
        return heads, tails

    def forward(coeffs):
        parts = [into(spread[:, 128 * k : 128 * k + heights[k]], coeffs[k]) for k in range(3)]
        coarse = times(jnp.concatenate(parts, axis=1), table[:width], table[width:], transposed=True)
        fine = five(coeffs[3], 0)[MARGIN : MARGIN + rows]
        return coarse + five(fine, 1)

    def strips(which, heads, tails):
        copies = []
        for j, (tile, d) in enumerate(((heads, n_lat - 1), (tails, 1))):
            coarse = roll(jnp.concatenate(tile[:3], axis=1), 2, 0)
            fine = roll(tile[3], -2, 0)
            strip_send[which, j, :, :width] = jnp.where(above, coarse[:, :width], fine)
            strip_send[which, j, :, width:] = coarse[:, width:]
            copies.append(
                pltpu.make_async_remote_copy(
                    src_ref=strip_send.at[which, j],
                    dst_ref=strip_recv.at[which, j],
                    send_sem=strip_sem.at[4 * which + 2 * j],
                    recv_sem=strip_sem.at[4 * which + 2 * j + 1],
                    device_id={"lat": lat_peer(d)},
                    device_id_type=MESH,
                )
            )
            copies[-1].start()
        return copies

    def received(which, j, has):
        packed = strip_recv[which, j] * has
        coarse = jnp.where(summed, roll(packed, -2, 0), 0.0)
        fine = jnp.where(summed, roll(packed[:, :width], 2, 0), 0.0)
        return [coarse[:, span(k)] for k in range(3)] + [fine]

    def joined(which, extra=None):
        above_it = received(which, 1, jnp.where(lat > 0, 1.0, 0.0))
        below_it = received(which, 0, jnp.where(lat < n_lat - 1, 1.0, 0.0))
        result = []
        for k in range(LEVELS):
            partial = part_ref[k][...]
            if extra:
                partial = partial + extra[k]
            head = partial[:8] + above_it[k]
            tail = partial[heights[k] - 8 :] + below_it[k]
            middle = partial[8 : heights[k] - 8]
            result.append(jnp.concatenate([head, middle, tail], axis=0) * valid[k])
        return result

    def send_swaths(which):
        for e in order:
            peer = lon_partner(e)
            pltpu.make_async_remote_copy(
                src_ref=swath_src.at[which, pl.ds(pl.multiple_of(peer * swath, 8), swath), :],
                dst_ref=swath_dst.at[which, :, pl.ds(pl.multiple_of(lon * cols, 128), cols)],
                send_sem=swath_sem.at[2 * which],
                recv_sem=swath_sem.at[2 * which + 1],
                device_id={"lon": peer},
                device_id_type=MESH,
            ).start()
        at = pl.ds(pl.multiple_of(lon * cols, 128), cols)
        swath_dst[which, :, at] = swath_src[which, own, :]

    def extract(k, x):
        s = SPACINGS[k]
        return x[MARGIN : MARGIN + rows // s, HALO // s : HALO // s + cols // s]


    def squares(k, x):
        y = x * x
        n = heights[k]
        ends = jnp.where(above, y[:8], 0.0) + jnp.where(above, 0.0, y[n - 8 :])
        return fold_lanes((fold(y[8 : n - 8]) + ends) * inside[k])

    lane = lax.broadcasted_iota(jnp.int32, (1, width), 1)
    own_lane = jnp.where((lane >= HALO) & (lane < HALO + cols), 1.0, 0.0)

    def misfits(surface):
        misfit = 2.0 * gau_pad[...] * surface
        return misfit, fold_lanes(fold(misfit * surface) * own_lane)

    misfit = 2.0 * gau_pad[...] * obs_tile[...]
    copies = strips(0, *adjoint_edges(misfit))

    @pl.when(lat >= 0)
    def _():
        adjoint(2.0 * gau_pad[...] * obs_tile[...])

    for copy in copies:
        copy.wait()
    right = joined(0)

    surface = forward(right)
    surface_ref[...] = surface
    heads, tails = adjoint_edges(2.0 * gau_pad[...] * surface)
    for k in range(LEVELS):
        n = heights[k]
        for tile, x, ok, own_rows in (
            (heads, right[k][:8], valid[k][:8], above),
            (tails, right[k][n - 8 :], valid[k][n - 8 :], ~above),
        ):
            tile[k] = tile[k] + SCALES[k] * stencil(stencil(jnp.where(own_rows, x, 0.0)) * ok)
    copies = strips(1, heads, tails)
    for k in range(LEVELS):
        right_ref[k][...] = right[k]

    @pl.when(lat >= 0)
    def _():
        misfit, mu1 = misfits(surface_ref[...])
        adjoint(misfit)
        mu0 = jnp.zeros((8, 128), F32)
        for k in range(LEVELS):
            x = right_ref[k][...]
            n = heights[k]
            head, tail = jnp.where(above, x[:8], 0.0), jnp.where(above, 0.0, x[n - 8 :])
            own_x = jnp.concatenate([head, x[8 : n - 8], tail], axis=0)
            part_ref[k][...] += SCALES[k] * stencil(stencil(own_x) * valid[k])
            mu0 = mu0 + squares(k, x)
            mu1 = mu1 + SCALES[k] * squares(k, stencil(x) * valid[k])
        mu_ref[0] = mu0
        mu_ref[1] = mu1

    for copy in copies:
        copy.wait()
    image = joined(1)

    surface = forward(image)
    mu2 = jnp.zeros((8, 128), F32)
    _, mu3 = misfits(surface)
    for k in range(LEVELS):
        mu2 = mu2 + squares(k, image[k])
        mu3 = mu3 + SCALES[k] * squares(k, stencil(image[k]) * valid[k])

    sub8 = lax.broadcasted_iota(jnp.int32, (8, 128), 0)
    lane8 = lax.broadcasted_iota(jnp.int32, (8, 128), 1)

    def reduce_start(stage, value, dst, sem, order, peer_of):
        red_src[stage] = value
        for d in order:
            pltpu.make_async_remote_copy(
                src_ref=red_src.at[stage],
                dst_ref=dst.at[d - 1],
                send_sem=sem.at[0],
                recv_sem=sem.at[1],
                device_id=peer_of(d),
                device_id_type=MESH,
            ).start()

    def reduce_end(value, dst, sem):
        pltpu.make_async_copy(dst, dst, sem.at[1]).wait()
        return value + jnp.sum(dst[...], axis=0)

    gathered = jnp.zeros((8, 128), F32)
    for i, value in enumerate((mu_ref[0], mu_ref[1], mu2, mu3)):
        gathered = gathered + jnp.where(sub8 == i, jnp.sum(value, axis=0, keepdims=True), 0.0)
    gathered = jnp.sum(gathered, axis=1, keepdims=True)
    moments = jnp.sum(jnp.where(sub8 == lane8, gathered, 0.0), axis=0, keepdims=True)
    reduce_start(0, moments, red_plane, plane_sem, plane, plane_peer)
    swath_src[0] = surface_ref[:, HALO : HALO + cols]
    send_swaths(0)
    swath_src[1] = surface[:, HALO : HALO + cols]
    for k in range(LEVELS):
        r_out[k][...] = extract(k, right_ref[k][...])
        q_out[k][...] = extract(k, image[k])
    moments = reduce_end(moments, red_plane, plane_sem)
    pl.semaphore_wait(line_ready, 2)
    reduce_start(1, moments, red_line, line_sem, line, line_peer)
    send_swaths(1)
    everything = swath_dst.at[0, :, : (n_lon - 1) * cols]
    for which, out in ((0, first_out), (1, second_out)):
        pltpu.make_async_copy(everything, everything, swath_sem.at[2 * which + 1]).wait()
        out[...] = swath_dst[which]
    moments = reduce_end(moments, red_line, line_sem)

    m0, m1, m2, m3 = (moments[:, i : i + 1] for i in range(4))
    alpha = m0 / m1
    grow = alpha * m2 / m1
    second_norm = alpha * alpha * m2 - m0
    curv = alpha * alpha * m3 - grow * grow * m1
    gamma = second_norm / curv
    lane1 = lane8[:1]
    mix_out[...] = jnp.where(lane1 == 0, alpha + gamma * grow, 0.0) + jnp.where(lane1 == 1, -alpha * gamma, 0.0)

    for which in range(2):
        pltpu.make_async_copy(everything, everything, swath_sem.at[2 * which]).wait()
    pltpu.make_async_copy(red_plane, red_plane, plane_sem.at[0]).wait()
    pltpu.make_async_copy(red_line, red_line, line_sem.at[0]).wait()


def combine(*refs):
    mix = refs[0][...]
    a, b = mix[:, 0:1], mix[:, 1:2]
    count = LEVELS + 1
    for first, second, out in zip(refs[1 : 1 + count], refs[1 + count : 1 + 2 * count], refs[1 + 2 * count :]):
        out[...] = a * first[...] + b * second[...]


def body(observed, gauged):
    n_lat, n_lon = lax.axis_size("lat"), lax.axis_size("lon")
    rows, cols = gauged.shape
    swath = observed.shape[0]
    width = cols + 2 * HALO
    back, edge, spread, table = tables(rows, cols)
    level_shapes = [jax.ShapeDtypeStruct((rows // s, cols // s), F32) for s in SPACINGS]
    swath_shape = jax.ShapeDtypeStruct(observed.shape, F32)
    node_shapes = [pltpu.VMEM((rows // s + 2 * MARGIN, lanes_of(width, s)), F32) for s in SPACINGS]
    vmem = pl.BlockSpec(memory_space=pltpu.VMEM)
    anywhere = pl.BlockSpec(memory_space=pl.ANY)
    dma = pltpu.SemaphoreType.DMA
    *pieces, mix = pl.pallas_call(
        functools.partial(kernel, n_lat, n_lon),
        out_shape=[pltpu.VMEM(x.shape, F32) for x in (*level_shapes, *level_shapes, swath_shape, swath_shape)]
        + [pltpu.VMEM((1, 128), F32)],
        in_specs=[anywhere] * 6,
        out_specs=[vmem] * 11,
        scratch_shapes=[
            pltpu.VMEM(observed.shape, F32),
            pltpu.VMEM(gauged.shape, gauged.dtype),
            pltpu.VMEM(back.shape, BF16),
            pltpu.VMEM(edge.shape, BF16),
            pltpu.VMEM(spread.shape, BF16),
            pltpu.VMEM(table.shape, BF16),
            pltpu.VMEM((swath, n_lon * cols + 2 * HALO), F32),
            pltpu.VMEM((rows, width), F32),
            pltpu.VMEM((rows, width), F32),
            pltpu.VMEM((2, rows // 2, 128), F32),
            pltpu.VMEM((2, rows // 2, 128), F32),
            pltpu.VMEM((rows + 2 * MARGIN, width), F32),
            *node_shapes,
            *node_shapes,
            pltpu.VMEM((rows, width), F32),
            pltpu.VMEM((2, 8, 128), F32),
            *[pltpu.VMEM((2, 2, 8, sum(lanes_of(width, s) for s in SPACINGS[:3])), F32)] * 2,
            pltpu.VMEM((2, rows, cols), F32),
            pltpu.VMEM((2, swath, n_lon * cols), F32),
            pltpu.VMEM((2, 1, 128), F32),
            pltpu.VMEM((2 * n_lon - 1, 1, 128), F32),
            pltpu.VMEM((n_lat // 2 - 1, 1, 128), F32),
            dma((6,)),
            dma((2,)),
            dma((4,)),
            dma((8,)),
            dma((4,)),
            dma((2,)),
            dma((2,)),
            pltpu.SemaphoreType.REGULAR,
        ],
        compiler_params=pltpu.CompilerParams(collective_id=0, has_side_effects=True),
        name="krylov",
    )(observed, gauged, back, edge, spread, table)
    mix, *pieces = [pltpu.with_memory_space_constraint(x, pltpu.VMEM) for x in (mix, *pieces)]
    firsts = [*pieces[:LEVELS], pieces[2 * LEVELS]]
    seconds = [*pieces[LEVELS : 2 * LEVELS], pieces[2 * LEVELS + 1]]
    return pl.pallas_call(
        combine,
        out_shape=(*level_shapes, swath_shape),
        in_specs=[vmem] * 11,
        out_specs=[vmem] * 5,
        name="combine",
    )(mix, *firsts, *seconds)


def solution(mesh):
    tile = P("lat", "lon")
    swaths = P(("lat", "lon"), None)
    return jax.shard_map(
        body,
        mesh=mesh,
        in_specs=(swaths, tile),
        out_specs=(tile, tile, tile, tile, swaths),
        check_vma=False,
    )
```

```python
import functools
import math

import jax
import jax.numpy as jnp
import numpy as np
from jax import lax
from jax.experimental import pallas as pl
from jax.experimental.pallas import tpu as pltpu
from jax.sharding import PartitionSpec as P

LEVELS = 4
SPACINGS = (8, 4, 2, 1)
SCALES = (0.02, 0.03, 0.05, 0.08)
HALO = 64
MARGIN = 4
MESH = pl.DeviceIdType.MESH
F32 = jnp.float32
BF16 = jnp.bfloat16


def weight(cells, nodes, spacing):
    numerator = np.abs(2 * cells - 2 * spacing * nodes - (spacing - 1))
    d = numerator / (5.0 * spacing)
    value = np.maximum(1.0 - d, 0.0) ** 6 * (35.0 * d * d + 18.0 * d + 3.0) / 3.0
    return value / math.sqrt(spacing)


def halves(table):
    table = np.asarray(table, np.float32)
    high = table.astype(BF16)
    low = (table - high.astype(np.float32)).astype(BF16)
    return jnp.asarray(np.concatenate([high, low], axis=0))


def lanes_of(width, spacing):
    return -(-(width // spacing) // 128) * 128


def tables(rows, cols):
    width = cols + 2 * HALO
    row_parts, col_parts = [], []
    for s in SPACINGS[:3]:
        nodes = np.arange(rows // s + 2 * MARGIN) - MARGIN
        row_parts.append(weight(np.arange(rows)[None, :], nodes[:, None], s))
        nodes = np.arange(width // s) - HALO // s
        part = np.zeros((width, lanes_of(width, s)))
        part[:, : width // s] = weight(np.arange(width)[:, None] - HALO, nodes[None, :], s)
        col_parts.append(part)
    back = np.concatenate(row_parts, axis=0)
    spread = np.zeros((rows, 128 * len(row_parts)))
    for k, part in enumerate(row_parts):
        spread[:, 128 * k : 128 * k + part.shape[0]] = part.T
    edges = [x for part in row_parts for x in (part[:8], part[-8:])]
    return halves(back), halves(np.concatenate(edges)), halves(spread), halves(np.concatenate(col_parts, axis=1))


def halve(x):
    high = x.astype(BF16).astype(F32)
    return jnp.concatenate([high, x - high], axis=0).astype(BF16)


def times(x, high, low, transposed=False):
    contract = (((1,), (1 if transposed else 0,)), ((), ()))
    n = x.shape[0]
    x = halve(x)
    both = lax.dot_general(x, high, contract, preferred_element_type=F32)
    rest = lax.dot_general(x[:n], low, contract, preferred_element_type=F32)
    return both[:n] + both[n:] + rest


def into(table, x):
    n = table.shape[0] // 2
    high = x.astype(BF16)
    low = (x - high.astype(F32)).astype(BF16)
    both = jnp.dot(table, high, preferred_element_type=F32)
    rest = jnp.dot(table[:n], low, preferred_element_type=F32)
    return both[:n] + both[n:] + rest


def roll(x, shift, axis):
    return pltpu.roll(x, shift % x.shape[axis], axis)


TAPS = [float(np.float32(weight(np.int64(0), np.int64(o), 1))) for o in range(3)]


def five(x, axis):
    near = roll(x, 1, axis) + roll(x, -1, axis)
    far = roll(x, 2, axis) + roll(x, -2, axis)
    return TAPS[0] * x + TAPS[1] * near + TAPS[2] * far


def stencil(x):
    return 5.0 * x - (roll(x, 1, 0) + roll(x, -1, 0) + roll(x, 1, 1) + roll(x, -1, 1))


def fold(x):
    return jnp.sum(x.reshape(x.shape[0] // 8, 8, x.shape[1]), axis=0)


def fold_lanes(x):
    result = x[:, :128]
    for at in range(128, x.shape[1], 128):
        result = result + x[:, at : at + 128]
    return result


def kernel(n_lat, n_lon, *refs):
    (
        obs_hbm, gau_hbm, back_hbm, edge_hbm, spread_hbm, cols_hbm,
        r0_out, r1_out, r2_out, r3_out, q0_out, q1_out, q2_out, q3_out, first_out, second_out, mix_out,
        obs_ref, gau_ref, back, edge, spread, table, obs_pad, obs_tile, gau_pad, gau_send, gau_recv, extended,
        part0, part1, part2, part3, right0, right1, right2, right3, surface_ref, mu_ref, strip_send, strip_recv, swath_src, swath_dst, red_src, red_plane, red_line,
        load_sem, obs_sem, gau_sem, strip_sem, swath_sem, plane_sem, line_sem, line_ready,
    ) = refs
    part_ref = (part0, part1, part2, part3)
    right_ref = (right0, right1, right2, right3)
    r_out = (r0_out, r1_out, r2_out, r3_out)
    q_out = (q0_out, q1_out, q2_out, q3_out)
    lat, lon = lax.axis_index("lat"), lax.axis_index("lon")
    rows, cols = gau_hbm.shape
    width = cols + 2 * HALO
    swath = obs_hbm.shape[0]
    lanes = [lanes_of(width, s) for s in SPACINGS]
    starts = [sum(lanes[:k]) for k in range(LEVELS)]
    heights = [rows // s + 2 * MARGIN for s in SPACINGS]
    tops = [sum(heights[:k]) for k in range(LEVELS)]

    def lon_peer(d):
        return lax.rem(lon + d, n_lon)

    def lon_partner(e):
        peer = lon
        for b in (1, 2, 4, 8):
            if e & b and b < n_lon:
                peer = peer + b - 2 * b * lax.rem(lon // b, 2)
        return peer

    order = sorted(range(1, n_lon), key=lambda e: (-(e & 2), -(e & 12), e & 1))

    def lat_peer(d):
        return lax.rem(lat + d, n_lat)

    twin = lat + 1 - 2 * lax.rem(lat, 2)

    def plane_peer(e):
        return {"lat": twin if e >= n_lon else lat, "lon": lon_peer(e)}

    def line_peer(f):
        return {"lat": lat_peer(2 * f)}

    loads = [
        pltpu.make_async_copy(src, dst, load_sem.at[i])
        for i, (src, dst) in enumerate(
            (
                (obs_hbm, obs_ref),
                (gau_hbm, gau_ref),
                (edge_hbm, edge),
                (cols_hbm, table),
                (back_hbm, back),
                (spread_hbm, spread),
            )
        )
    ]
    for load in loads:
        load.start()

    valid = []
    inside = []
    for k, s in enumerate(SPACINGS):
        row = lax.broadcasted_iota(jnp.int32, (heights[k], 1), 0) - MARGIN
        col = lax.broadcasted_iota(jnp.int32, (1, lanes[k]), 1) - HALO // s
        row_global, col_global = row + lat * (rows // s), col + lon * (cols // s)
        row_ok = jnp.where((row_global >= 0) & (row_global < n_lat * (rows // s)), 1.0, 0.0)
        col_ok = jnp.where((col_global >= 0) & (col_global < n_lon * (cols // s)), 1.0, 0.0)
        valid.append(row_ok * col_ok)
        inside.append(jnp.where((col >= 0) & (col < cols // s), 1.0, 0.0))

    barrier = pltpu.get_barrier_semaphore()
    beyond = {"lat": lax.rem(lat + n_lat - 1 + 2 * lax.rem(lat, 2), n_lat)}
    planes = n_lat // 2
    line = sorted(range(1, planes), key=lambda f: abs(f - planes // 2))
    reach = max(planes // 4, 1)
    near = [f for f in line if min(f, planes - f) <= reach]
    plane = sorted(range(1, 2 * n_lon), key=lambda e: abs(e % n_lon - n_lon // 2))
    for f in near:
        pl.semaphore_signal(barrier, inc=1, device_id=line_peer(f), device_id_type=MESH)
    for e in plane:
        pl.semaphore_signal(barrier, inc=1, device_id=plane_peer(e), device_id_type=MESH)
    pl.semaphore_signal(barrier, inc=1, device_id=beyond, device_id_type=MESH)

    extended[...] = jnp.zeros_like(extended)
    loads[0].wait()
    loads[1].wait()
    obs_pad[:, :128] = jnp.zeros((swath, 128), F32)
    obs_pad[:, n_lon * cols :] = jnp.zeros((swath, 128), F32)
    obs_pad[:, HALO : HALO + n_lon * cols] = obs_ref[...]
    gau_pad[:, :128] = jnp.zeros((rows, 128), F32)
    gau_pad[:, cols:] = jnp.zeros((rows, 128), F32)
    gauge = gau_ref[...].astype(F32)
    gau_pad[:, HALO : HALO + cols] = gauge
    half = rows // 2
    lane = lax.broadcasted_iota(jnp.int32, (half, 128), 1)
    last, first = gauge[:, cols - 128 :], gauge[:, :128]
    gau_send[0] = jnp.where(lane < HALO, roll(last[:half], HALO, 1), last[half:])
    gau_send[1] = jnp.where(lane < HALO, first[:half], roll(first[half:], HALO, 1))

    pl.semaphore_wait(barrier, len(near) + 1 + 2 * n_lon - 1)
    for f in (reach, planes - reach):
        pl.semaphore_signal(line_ready, inc=1, device_id=line_peer(f), device_id_type=MESH)

    def scatter(e):
        peer = lon_partner(e)
        pltpu.make_async_remote_copy(
            src_ref=obs_pad.at[:, pl.ds(pl.multiple_of(peer * cols, 128), width)],
            dst_ref=obs_tile.at[pl.ds(pl.multiple_of(lon * swath, 8), swath), :],
            send_sem=obs_sem.at[0],
            recv_sem=obs_sem.at[1],
            device_id={"lon": peer},
            device_id_type=MESH,
        ).start()

    def finish(copy, sends, gets):
        pl.when(sends)(lambda: copy.wait_send())
        pl.when(gets)(lambda: copy.wait_recv())

    has_up, has_down = lat > 0, lat < n_lat - 1

    @pl.when(lon == 0)
    def _():
        gau_recv[0] = jnp.zeros_like(gau_recv[0])

    @pl.when(lon == n_lon - 1)
    def _():
        gau_recv[1] = jnp.zeros_like(gau_recv[1])

    @pl.when(lat == 0)
    def _():
        strip_recv[:, 1] = jnp.zeros_like(strip_recv[:, 1])

    @pl.when(lat == n_lat - 1)
    def _():
        strip_recv[:, 0] = jnp.zeros_like(strip_recv[:, 0])

    def beside(which, d):
        return pltpu.make_async_remote_copy(
            src_ref=gau_send.at[which],
            dst_ref=gau_recv.at[which],
            send_sem=gau_sem.at[2 * which],
            recv_sem=gau_sem.at[2 * which + 1],
            device_id={"lon": lon_peer(d)},
            device_id_type=MESH,
        )

    has_left, has_right = lon > 0, lon < n_lon - 1
    to_right, to_left = beside(0, 1), beside(1, n_lon - 1)
    for e in order:
        scatter(e)
    pl.when(has_right)(lambda: to_right.start())
    pl.when(has_left)(lambda: to_left.start())
    own = pl.ds(pl.multiple_of(lon * swath, 8), swath)
    obs_tile[own, :] = obs_pad[:, pl.ds(pl.multiple_of(lon * cols, 128), width)]

    for load in loads[2:]:
        load.wait()
    finish(to_right, has_right, has_left)
    finish(to_left, has_left, has_right)
    packed = gau_recv[0]
    gau_pad[:half, :128] = jnp.where(lane < HALO, packed, gau_pad[:half, :128])
    gau_pad[half:, :128] = jnp.where(lane < HALO, roll(packed, HALO, 1), gau_pad[half:, :128])
    packed = gau_recv[1]
    gau_pad[:half, cols:] = jnp.where(lane < HALO, gau_pad[:half, cols:], roll(packed, HALO, 1))
    gau_pad[half:, cols:] = jnp.where(lane < HALO, gau_pad[half:, cols:], packed)
    all_obs = obs_tile.at[: (n_lon - 1) * swath]
    pltpu.make_async_copy(all_obs, all_obs, obs_sem.at[1]).wait()
    pltpu.make_async_copy(all_obs, all_obs, obs_sem.at[0]).wait()

    row8 = lax.broadcasted_iota(jnp.int32, (8, 1), 0)
    above = row8 >= MARGIN
    summed = (row8 >= 2) & (row8 < 6)

    def span(k):
        return slice(starts[k], starts[k] + lanes[k])

    def adjoint(misfit):
        part = into(back[...], misfit)
        for k in range(3):
            rows_k = part[tops[k] : tops[k] + heights[k]]
            part_ref[k][...] = times(rows_k, table[:width, span(k)], table[width:, span(k)])
        extended[MARGIN : MARGIN + rows, :] = five(misfit, 1)
        part3[...] = five(extended[...], 0)

    def adjoint_edges(misfit):
        part = into(edge[...], misfit)
        heads, tails = [], []
        for k in range(3):
            both = times(part[16 * k : 16 * k + 16], table[:width, span(k)], table[width:, span(k)])
            heads.append(both[:8])
            tails.append(both[8:])
        near, away = five(misfit[:8], 1), five(misfit[rows - 8 :], 1)
        heads.append(five(jnp.where(above, roll(near, 4, 0), 0.0), 0))
        tails.append(five(jnp.where(above, 0.0, roll(away, 4, 0)), 0))
        return heads, tails

    def forward(coeffs):
        parts = [into(spread[:, 128 * k : 128 * k + heights[k]], coeffs[k]) for k in range(3)]
        coarse = times(jnp.concatenate(parts, axis=1), table[:width], table[width:], transposed=True)
        fine = five(coeffs[3], 0)[MARGIN : MARGIN + rows]
        return coarse + five(fine, 1)

    def strips(which, heads, tails):
        copies = []
        for j, (tile, d, sends, gets) in enumerate(
            ((heads, n_lat - 1, has_up, has_down), (tails, 1, has_down, has_up))
        ):
            coarse = roll(jnp.concatenate(tile[:3], axis=1), 2, 0)
            fine = roll(tile[3], -2, 0)
            strip_send[which, j, :, :width] = jnp.where(above, coarse[:, :width], fine)
            strip_send[which, j, :, width:] = coarse[:, width:]
            copy = pltpu.make_async_remote_copy(
                src_ref=strip_send.at[which, j],
                dst_ref=strip_recv.at[which, j],
                send_sem=strip_sem.at[4 * which + 2 * j],
                recv_sem=strip_sem.at[4 * which + 2 * j + 1],
                device_id={"lat": lat_peer(d)},
                device_id_type=MESH,
            )
            copies.append((copy, sends, gets))
        for copy, sends, _ in copies:
            pl.when(sends)(lambda: copy.start())
        return copies

    def received(which, j):
        packed = strip_recv[which, j]
        coarse = jnp.where(summed, roll(packed, -2, 0), 0.0)
        fine = jnp.where(summed, roll(packed[:, :width], 2, 0), 0.0)
        return [coarse[:, span(k)] for k in range(3)] + [fine]

    def joined(which, extra=None):
        above_it = received(which, 1)
        below_it = received(which, 0)
        result = []
        for k in range(LEVELS):
            partial = part_ref[k][...]
            if extra:
                partial = partial + extra[k]
            head = partial[:8] + above_it[k]
            tail = partial[heights[k] - 8 :] + below_it[k]
            middle = partial[8 : heights[k] - 8]
            result.append(jnp.concatenate([head, middle, tail], axis=0) * valid[k])
        return result

    def send_swaths(which):
        for e in order:
            peer = lon_partner(e)
            pltpu.make_async_remote_copy(
                src_ref=swath_src.at[which, pl.ds(pl.multiple_of(peer * swath, 8), swath), :],
                dst_ref=swath_dst.at[which, :, pl.ds(pl.multiple_of(lon * cols, 128), cols)],
                send_sem=swath_sem.at[2 * which],
                recv_sem=swath_sem.at[2 * which + 1],
                device_id={"lon": peer},
                device_id_type=MESH,
            ).start()
        at = pl.ds(pl.multiple_of(lon * cols, 128), cols)
        swath_dst[which, :, at] = swath_src[which, own, :]

    def extract(k, x):
        s = SPACINGS[k]
        return x[MARGIN : MARGIN + rows // s, HALO // s : HALO // s + cols // s]


    def squares(k, x):
        y = x * x
        n = heights[k]
        ends = jnp.where(above, y[:8], 0.0) + jnp.where(above, 0.0, y[n - 8 :])
        return fold_lanes((fold(y[8 : n - 8]) + ends) * inside[k])

    lane = lax.broadcasted_iota(jnp.int32, (1, width), 1)
    own_lane = jnp.where((lane >= HALO) & (lane < HALO + cols), 1.0, 0.0)

    def misfits(surface):
        misfit = 2.0 * gau_pad[...] * surface
        return misfit, fold_lanes(fold(misfit * surface) * own_lane)

    misfit = 2.0 * gau_pad[...] * obs_tile[...]
    copies = strips(0, *adjoint_edges(misfit))

    @pl.when(lat >= 0)
    def _():
        adjoint(2.0 * gau_pad[...] * obs_tile[...])

    for copy in copies:
        finish(*copy)
    right = joined(0)

    surface = forward(right)
    surface_ref[...] = surface
    heads, tails = adjoint_edges(2.0 * gau_pad[...] * surface)
    for k in range(LEVELS):
        n = heights[k]
        for tile, x, ok, own_rows in (
            (heads, right[k][:8], valid[k][:8], above),
            (tails, right[k][n - 8 :], valid[k][n - 8 :], ~above),
        ):
            tile[k] = tile[k] + SCALES[k] * stencil(stencil(jnp.where(own_rows, x, 0.0)) * ok)
    copies = strips(1, heads, tails)
    for k in range(LEVELS):
        right_ref[k][...] = right[k]

    @pl.when(lat >= 0)
    def _():
        misfit, mu1 = misfits(surface_ref[...])
        adjoint(misfit)
        mu0 = jnp.zeros((8, 128), F32)
        for k in range(LEVELS):
            x = right_ref[k][...]
            n = heights[k]
            head, tail = jnp.where(above, x[:8], 0.0), jnp.where(above, 0.0, x[n - 8 :])
            own_x = jnp.concatenate([head, x[8 : n - 8], tail], axis=0)
            part_ref[k][...] += SCALES[k] * stencil(stencil(own_x) * valid[k])
            mu0 = mu0 + squares(k, x)
            mu1 = mu1 + SCALES[k] * squares(k, stencil(x) * valid[k])
        mu_ref[0] = mu0
        mu_ref[1] = mu1

    for copy in copies:
        finish(*copy)
    image = joined(1)

    surface = forward(image)
    mu2 = jnp.zeros((8, 128), F32)
    _, mu3 = misfits(surface)
    for k in range(LEVELS):
        mu2 = mu2 + squares(k, image[k])
        mu3 = mu3 + SCALES[k] * squares(k, stencil(image[k]) * valid[k])

    sub8 = lax.broadcasted_iota(jnp.int32, (8, 128), 0)
    lane8 = lax.broadcasted_iota(jnp.int32, (8, 128), 1)

    def reduce_start(stage, value, dst, sem, order, peer_of):
        red_src[stage] = value
        for d in order:
            pltpu.make_async_remote_copy(
                src_ref=red_src.at[stage],
                dst_ref=dst.at[d - 1],
                send_sem=sem.at[0],
                recv_sem=sem.at[1],
                device_id=peer_of(d),
                device_id_type=MESH,
            ).start()

    def reduce_end(value, dst, sem):
        pltpu.make_async_copy(dst, dst, sem.at[1]).wait()
        return value + jnp.sum(dst[...], axis=0)

    gathered = jnp.zeros((8, 128), F32)
    for i, value in enumerate((mu_ref[0], mu_ref[1], mu2, mu3)):
        gathered = gathered + jnp.where(sub8 == i, jnp.sum(value, axis=0, keepdims=True), 0.0)
    gathered = jnp.sum(gathered, axis=1, keepdims=True)
    moments = jnp.sum(jnp.where(sub8 == lane8, gathered, 0.0), axis=0, keepdims=True)
    reduce_start(0, moments, red_plane, plane_sem, plane, plane_peer)
    swath_src[0] = surface_ref[:, HALO : HALO + cols]
    send_swaths(0)
    swath_src[1] = surface[:, HALO : HALO + cols]
    for k in range(LEVELS):
        r_out[k][...] = extract(k, right_ref[k][...])
        q_out[k][...] = extract(k, image[k])
    moments = reduce_end(moments, red_plane, plane_sem)
    pl.semaphore_wait(line_ready, 2)
    reduce_start(1, moments, red_line, line_sem, line, line_peer)
    send_swaths(1)
    everything = swath_dst.at[0, :, : (n_lon - 1) * cols]
    for which, out in ((0, first_out), (1, second_out)):
        pltpu.make_async_copy(everything, everything, swath_sem.at[2 * which + 1]).wait()
        out[...] = swath_dst[which]
    moments = reduce_end(moments, red_line, line_sem)

    m0, m1, m2, m3 = (moments[:, i : i + 1] for i in range(4))
    alpha = m0 / m1
    grow = alpha * m2 / m1
    second_norm = alpha * alpha * m2 - m0
    curv = alpha * alpha * m3 - grow * grow * m1
    gamma = second_norm / curv
    lane1 = lane8[:1]
    mix_out[...] = jnp.where(lane1 == 0, alpha + gamma * grow, 0.0) + jnp.where(lane1 == 1, -alpha * gamma, 0.0)

    for which in range(2):
        pltpu.make_async_copy(everything, everything, swath_sem.at[2 * which]).wait()
    pltpu.make_async_copy(red_plane, red_plane, plane_sem.at[0]).wait()
    pltpu.make_async_copy(red_line, red_line, line_sem.at[0]).wait()


def combine(*refs):
    mix = refs[0][...]
    a, b = mix[:, 0:1], mix[:, 1:2]
    count = LEVELS + 1
    for first, second, out in zip(refs[1 : 1 + count], refs[1 + count : 1 + 2 * count], refs[1 + 2 * count :]):
        out[...] = a * first[...] + b * second[...]


def body(observed, gauged):
    n_lat, n_lon = lax.axis_size("lat"), lax.axis_size("lon")
    rows, cols = gauged.shape
    swath = observed.shape[0]
    width = cols + 2 * HALO
    back, edge, spread, table = tables(rows, cols)
    level_shapes = [jax.ShapeDtypeStruct((rows // s, cols // s), F32) for s in SPACINGS]
    swath_shape = jax.ShapeDtypeStruct(observed.shape, F32)
    node_shapes = [pltpu.VMEM((rows // s + 2 * MARGIN, lanes_of(width, s)), F32) for s in SPACINGS]
    vmem = pl.BlockSpec(memory_space=pltpu.VMEM)
    anywhere = pl.BlockSpec(memory_space=pl.ANY)
    dma = pltpu.SemaphoreType.DMA
    *pieces, mix = pl.pallas_call(
        functools.partial(kernel, n_lat, n_lon),
        out_shape=[pltpu.VMEM(x.shape, F32) for x in (*level_shapes, *level_shapes, swath_shape, swath_shape)]
        + [pltpu.VMEM((1, 128), F32)],
        in_specs=[anywhere] * 6,
        out_specs=[vmem] * 11,
        scratch_shapes=[
            pltpu.VMEM(observed.shape, F32),
            pltpu.VMEM(gauged.shape, gauged.dtype),
            pltpu.VMEM(back.shape, BF16),
            pltpu.VMEM(edge.shape, BF16),
            pltpu.VMEM(spread.shape, BF16),
            pltpu.VMEM(table.shape, BF16),
            pltpu.VMEM((swath, n_lon * cols + 2 * HALO), F32),
            pltpu.VMEM((rows, width), F32),
            pltpu.VMEM((rows, width), F32),
            pltpu.VMEM((2, rows // 2, 128), F32),
            pltpu.VMEM((2, rows // 2, 128), F32),
            pltpu.VMEM((rows + 2 * MARGIN, width), F32),
            *node_shapes,
            *node_shapes,
            pltpu.VMEM((rows, width), F32),
            pltpu.VMEM((2, 8, 128), F32),
            *[pltpu.VMEM((2, 2, 8, sum(lanes_of(width, s) for s in SPACINGS[:3])), F32)] * 2,
            pltpu.VMEM((2, rows, cols), F32),
            pltpu.VMEM((2, swath, n_lon * cols), F32),
            pltpu.VMEM((2, 1, 128), F32),
            pltpu.VMEM((2 * n_lon - 1, 1, 128), F32),
            pltpu.VMEM((n_lat // 2 - 1, 1, 128), F32),
            dma((6,)),
            dma((2,)),
            dma((4,)),
            dma((8,)),
            dma((4,)),
            dma((2,)),
            dma((2,)),
            pltpu.SemaphoreType.REGULAR,
        ],
        compiler_params=pltpu.CompilerParams(collective_id=0, has_side_effects=True),
        name="krylov",
    )(observed, gauged, back, edge, spread, table)
    mix, *pieces = [pltpu.with_memory_space_constraint(x, pltpu.VMEM) for x in (mix, *pieces)]
    firsts = [*pieces[:LEVELS], pieces[2 * LEVELS]]
    seconds = [*pieces[LEVELS : 2 * LEVELS], pieces[2 * LEVELS + 1]]
    return pl.pallas_call(
        combine,
        out_shape=(*level_shapes, swath_shape),
        in_specs=[vmem] * 11,
        out_specs=[vmem] * 5,
        name="combine",
    )(mix, *firsts, *seconds)


def solution(mesh):
    tile = P("lat", "lon")
    swaths = P(("lat", "lon"), None)
    return jax.shard_map(
        body,
        mesh=mesh,
        in_specs=(swaths, tile),
        out_specs=(tile, tile, tile, tile, swaths),
        check_vma=False,
    )
```

```python
import functools
import math

import jax
import jax.numpy as jnp
import numpy as np
from jax import lax
from jax.experimental import pallas as pl
from jax.experimental.pallas import tpu as pltpu
from jax.sharding import PartitionSpec as P

LEVELS = 4
SPACINGS = (8, 4, 2, 1)
SCALES = (0.02, 0.03, 0.05, 0.08)
HALO = 64
MARGIN = 4
MESH = pl.DeviceIdType.MESH
F32 = jnp.float32
BF16 = jnp.bfloat16


def weight(cells, nodes, spacing):
    numerator = np.abs(2 * cells - 2 * spacing * nodes - (spacing - 1))
    d = numerator / (5.0 * spacing)
    value = np.maximum(1.0 - d, 0.0) ** 6 * (35.0 * d * d + 18.0 * d + 3.0) / 3.0
    return value / math.sqrt(spacing)


def halves(table):
    table = np.asarray(table, np.float32)
    high = table.astype(BF16)
    low = (table - high.astype(np.float32)).astype(BF16)
    return jnp.asarray(np.concatenate([high, low], axis=0))


def lanes_of(width, spacing):
    return -(-(width // spacing) // 128) * 128


def tables(rows, cols):
    width = cols + 2 * HALO
    row_parts, col_parts = [], []
    for s in SPACINGS[:3]:
        nodes = np.arange(rows // s + 2 * MARGIN) - MARGIN
        row_parts.append(weight(np.arange(rows)[None, :], nodes[:, None], s))
        nodes = np.arange(width // s) - HALO // s
        part = np.zeros((width, lanes_of(width, s)))
        part[:, : width // s] = weight(np.arange(width)[:, None] - HALO, nodes[None, :], s)
        col_parts.append(part)
    back = np.concatenate(row_parts, axis=0)
    spread = np.zeros((rows, 128 * len(row_parts)))
    for k, part in enumerate(row_parts):
        spread[:, 128 * k : 128 * k + part.shape[0]] = part.T
    edges = [x for part in row_parts for x in (part[:8], part[-8:])]
    return halves(back), halves(np.concatenate(edges)), halves(spread), halves(np.concatenate(col_parts, axis=1))


def halve(x):
    high = x.astype(BF16).astype(F32)
    return jnp.concatenate([high, x - high], axis=0).astype(BF16)


def times(x, high, low, transposed=False):
    contract = (((1,), (1 if transposed else 0,)), ((), ()))
    n = x.shape[0]
    x = halve(x)
    both = lax.dot_general(x, high, contract, preferred_element_type=F32)
    rest = lax.dot_general(x[:n], low, contract, preferred_element_type=F32)
    return both[:n] + both[n:] + rest


def into(table, x):
    n = table.shape[0] // 2
    high = x.astype(BF16)
    low = (x - high.astype(F32)).astype(BF16)
    both = jnp.dot(table, high, preferred_element_type=F32)
    rest = jnp.dot(table[:n], low, preferred_element_type=F32)
    return both[:n] + both[n:] + rest


def roll(x, shift, axis):
    return pltpu.roll(x, shift % x.shape[axis], axis)


TAPS = [float(np.float32(weight(np.int64(0), np.int64(o), 1))) for o in range(3)]


def five(x, axis):
    near = roll(x, 1, axis) + roll(x, -1, axis)
    far = roll(x, 2, axis) + roll(x, -2, axis)
    return TAPS[0] * x + TAPS[1] * near + TAPS[2] * far


def stencil(x):
    return 5.0 * x - (roll(x, 1, 0) + roll(x, -1, 0) + roll(x, 1, 1) + roll(x, -1, 1))


def fold(x):
    return jnp.sum(x.reshape(x.shape[0] // 8, 8, x.shape[1]), axis=0)


def fold_lanes(x):
    result = x[:, :128]
    for at in range(128, x.shape[1], 128):
        result = result + x[:, at : at + 128]
    return result


def kernel(n_lat, n_lon, *refs):
    (
        obs_hbm, gau_hbm, back_hbm, edge_hbm, spread_hbm, cols_hbm,
        r0_out, r1_out, r2_out, r3_out, q0_out, q1_out, q2_out, q3_out, first_out, second_out, mix_out,
        obs_ref, gau_ref, back, edge, spread, table, obs_pad, obs_tile, gau_pad, gau_send, gau_recv, extended,
        part0, part1, part2, part3, right0, right1, right2, right3, surface_ref, mu_ref, strip_send, strip_recv, swath_src, swath_dst, red_src, red_plane, red_line,
        load_sem, obs_sem, gau_sem, strip_sem, swath_sem, plane_sem, line_sem, line_ready,
    ) = refs
    part_ref = (part0, part1, part2, part3)
    right_ref = (right0, right1, right2, right3)
    r_out = (r0_out, r1_out, r2_out, r3_out)
    q_out = (q0_out, q1_out, q2_out, q3_out)
    lat, lon = lax.axis_index("lat"), lax.axis_index("lon")
    rows, cols = gau_hbm.shape
    width = cols + 2 * HALO
    swath = obs_hbm.shape[0]
    lanes = [lanes_of(width, s) for s in SPACINGS]
    starts = [sum(lanes[:k]) for k in range(LEVELS)]
    heights = [rows // s + 2 * MARGIN for s in SPACINGS]
    tops = [sum(heights[:k]) for k in range(LEVELS)]

    def lon_peer(d):
        return lax.rem(lon + d, n_lon)

    def lon_partner(e):
        peer = lon
        for b in (1, 2, 4, 8):
            if e & b and b < n_lon:
                peer = peer + b - 2 * b * lax.rem(lon // b, 2)
        return peer

    order = sorted(range(1, n_lon), key=lambda e: (-(e & 2), -(e & 12), e & 1))

    def lat_peer(d):
        return lax.rem(lat + d, n_lat)

    twin = lat + 1 - 2 * lax.rem(lat, 2)

    def plane_peer(e):
        return {"lat": twin if e >= n_lon else lat, "lon": lon_peer(e)}

    def line_peer(f):
        return {"lat": lat_peer(2 * f)}

    loads = [
        pltpu.make_async_copy(src, dst, load_sem.at[i])
        for i, (src, dst) in enumerate(
            (
                (obs_hbm, obs_ref),
                (gau_hbm, gau_ref),
                (edge_hbm, edge),
                (cols_hbm, table),
                (back_hbm, back),
                (spread_hbm, spread),
            )
        )
    ]
    for load in loads:
        load.start()

    valid = []
    inside = []
    for k, s in enumerate(SPACINGS):
        row = lax.broadcasted_iota(jnp.int32, (heights[k], 1), 0) - MARGIN
        col = lax.broadcasted_iota(jnp.int32, (1, lanes[k]), 1) - HALO // s
        row_global, col_global = row + lat * (rows // s), col + lon * (cols // s)
        row_ok = jnp.where((row_global >= 0) & (row_global < n_lat * (rows // s)), 1.0, 0.0)
        col_ok = jnp.where((col_global >= 0) & (col_global < n_lon * (cols // s)), 1.0, 0.0)
        valid.append(row_ok * col_ok)
        inside.append(jnp.where((col >= 0) & (col < cols // s), 1.0, 0.0))

    barrier = pltpu.get_barrier_semaphore()
    beyond = {"lat": lax.rem(lat + n_lat - 1 + 2 * lax.rem(lat, 2), n_lat)}
    planes = n_lat // 2
    line = sorted(range(1, planes), key=lambda f: abs(f - planes // 2))
    reach = max(planes // 4, 1)
    near = [f for f in line if min(f, planes - f) <= reach]
    plane = sorted(range(1, 2 * n_lon), key=lambda e: abs(e % n_lon - n_lon // 2))
    for f in near:
        pl.semaphore_signal(barrier, inc=1, device_id=line_peer(f), device_id_type=MESH)
    for e in plane:
        pl.semaphore_signal(barrier, inc=1, device_id=plane_peer(e), device_id_type=MESH)
    pl.semaphore_signal(barrier, inc=1, device_id=beyond, device_id_type=MESH)

    extended[...] = jnp.zeros_like(extended)
    loads[0].wait()
    loads[1].wait()
    obs_pad[:, :128] = jnp.zeros((swath, 128), F32)
    obs_pad[:, n_lon * cols :] = jnp.zeros((swath, 128), F32)
    obs_pad[:, HALO : HALO + n_lon * cols] = obs_ref[...]
    gau_pad[:, :128] = jnp.zeros((rows, 128), F32)
    gau_pad[:, cols:] = jnp.zeros((rows, 128), F32)
    gauge = gau_ref[...].astype(F32)
    gau_pad[:, HALO : HALO + cols] = gauge
    half = rows // 2
    lane = lax.broadcasted_iota(jnp.int32, (half, 128), 1)
    last, first = gauge[:, cols - 128 :], gauge[:, :128]
    gau_send[0] = jnp.where(lane < HALO, roll(last[:half], HALO, 1), last[half:])
    gau_send[1] = jnp.where(lane < HALO, first[:half], roll(first[half:], HALO, 1))

    pl.semaphore_wait(barrier, len(near) + 1 + 2 * n_lon - 1)
    for f in (reach, planes - reach):
        pl.semaphore_signal(line_ready, inc=1, device_id=line_peer(f), device_id_type=MESH)

    def scatter(e):
        peer = lon_partner(e)
        pltpu.make_async_remote_copy(
            src_ref=obs_pad.at[:, pl.ds(pl.multiple_of(peer * cols, 128), width)],
            dst_ref=obs_tile.at[pl.ds(pl.multiple_of(lon * swath, 8), swath), :],
            send_sem=obs_sem.at[0],
            recv_sem=obs_sem.at[1],
            device_id={"lon": peer},
            device_id_type=MESH,
        ).start()

    def beside(which, d):
        return pltpu.make_async_remote_copy(
            src_ref=gau_send.at[which],
            dst_ref=gau_recv.at[which],
            send_sem=gau_sem.at[2 * which],
            recv_sem=gau_sem.at[2 * which + 1],
            device_id={"lon": lon_peer(d)},
            device_id_type=MESH,
        )

    to_right, to_left = beside(0, 1), beside(1, n_lon - 1)
    for e in order:
        scatter(e)
    to_right.start()
    to_left.start()
    own = pl.ds(pl.multiple_of(lon * swath, 8), swath)
    obs_tile[own, :] = obs_pad[:, pl.ds(pl.multiple_of(lon * cols, 128), width)]

    for load in loads[2:]:
        load.wait()
    to_right.wait()
    to_left.wait()
    packed = gau_recv[0] * jnp.where(lon > 0, 1.0, 0.0)
    gau_pad[:half, :128] = jnp.where(lane < HALO, packed, gau_pad[:half, :128])
    gau_pad[half:, :128] = jnp.where(lane < HALO, roll(packed, HALO, 1), gau_pad[half:, :128])
    packed = gau_recv[1] * jnp.where(lon < n_lon - 1, 1.0, 0.0)
    gau_pad[:half, cols:] = jnp.where(lane < HALO, gau_pad[:half, cols:], roll(packed, HALO, 1))
    gau_pad[half:, cols:] = jnp.where(lane < HALO, gau_pad[half:, cols:], packed)
    all_obs = obs_tile.at[: (n_lon - 1) * swath]
    pltpu.make_async_copy(all_obs, all_obs, obs_sem.at[1]).wait()
    pltpu.make_async_copy(all_obs, all_obs, obs_sem.at[0]).wait()

    row8 = lax.broadcasted_iota(jnp.int32, (8, 1), 0)
    above = row8 >= MARGIN
    summed = (row8 >= 2) & (row8 < 6)

    def span(k):
        return slice(starts[k], starts[k] + lanes[k])

    def adjoint(misfit):
        part = into(back[...], misfit)
        for k in range(3):
            rows_k = part[tops[k] : tops[k] + heights[k]]
            part_ref[k][...] = times(rows_k, table[:width, span(k)], table[width:, span(k)])
        extended[MARGIN : MARGIN + rows, :] = five(misfit, 1)
        part3[...] = five(extended[...], 0)

    def adjoint_edges(misfit):
        part = into(edge[...], misfit)
        heads, tails = [], []
        for k in range(3):
            both = times(part[16 * k : 16 * k + 16], table[:width, span(k)], table[width:, span(k)])
            heads.append(both[:8])
            tails.append(both[8:])
        near, away = five(misfit[:8], 1), five(misfit[rows - 8 :], 1)
        heads.append(five(jnp.where(above, roll(near, 4, 0), 0.0), 0))
        tails.append(five(jnp.where(above, 0.0, roll(away, 4, 0)), 0))
        return heads, tails

    def forward(coeffs):
        parts = [into(spread[:, 128 * k : 128 * k + heights[k]], coeffs[k]) for k in range(3)]
        coarse = times(jnp.concatenate(parts, axis=1), table[:width], table[width:], transposed=True)
        fine = five(coeffs[3], 0)[MARGIN : MARGIN + rows]
        return coarse + five(fine, 1)

    def strips(which, heads, tails):
        copies = []
        for j, (tile, d) in enumerate(((heads, n_lat - 1), (tails, 1))):
            coarse = roll(jnp.concatenate(tile[:3], axis=1), 2, 0)
            fine = roll(tile[3], -2, 0)
            strip_send[which, j, :, :width] = jnp.where(above, coarse[:, :width], fine)
            strip_send[which, j, :, width:] = coarse[:, width:]
            copies.append(
                pltpu.make_async_remote_copy(
                    src_ref=strip_send.at[which, j],
                    dst_ref=strip_recv.at[which, j],
                    send_sem=strip_sem.at[4 * which + 2 * j],
                    recv_sem=strip_sem.at[4 * which + 2 * j + 1],
                    device_id={"lat": lat_peer(d)},
                    device_id_type=MESH,
                )
            )
            copies[-1].start()
        return copies

    def received(which, j, has):
        packed = strip_recv[which, j] * has
        coarse = jnp.where(summed, roll(packed, -2, 0), 0.0)
        fine = jnp.where(summed, roll(packed[:, :width], 2, 0), 0.0)
        return [coarse[:, span(k)] for k in range(3)] + [fine]

    def joined(which, extra=None):
        above_it = received(which, 1, jnp.where(lat > 0, 1.0, 0.0))
        below_it = received(which, 0, jnp.where(lat < n_lat - 1, 1.0, 0.0))
        result = []
        for k in range(LEVELS):
            partial = part_ref[k][...]
            if extra:
                partial = partial + extra[k]
            head = partial[:8] + above_it[k]
            tail = partial[heights[k] - 8 :] + below_it[k]
            middle = partial[8 : heights[k] - 8]
            result.append(jnp.concatenate([head, middle, tail], axis=0) * valid[k])
        return result

    def send_swaths(which):
        for e in order:
            peer = lon_partner(e)
            pltpu.make_async_remote_copy(
                src_ref=swath_src.at[which, pl.ds(pl.multiple_of(peer * swath, 8), swath), :],
                dst_ref=swath_dst.at[which, :, pl.ds(pl.multiple_of(lon * cols, 128), cols)],
                send_sem=swath_sem.at[2 * which],
                recv_sem=swath_sem.at[2 * which + 1],
                device_id={"lon": peer},
                device_id_type=MESH,
            ).start()
        at = pl.ds(pl.multiple_of(lon * cols, 128), cols)
        swath_dst[which, :, at] = swath_src[which, own, :]

    def extract(k, x):
        s = SPACINGS[k]
        return x[MARGIN : MARGIN + rows // s, HALO // s : HALO // s + cols // s]


    def squares(k, x):
        y = x * x
        n = heights[k]
        ends = jnp.where(above, y[:8], 0.0) + jnp.where(above, 0.0, y[n - 8 :])
        return fold_lanes((fold(y[8 : n - 8]) + ends) * inside[k])

    lane = lax.broadcasted_iota(jnp.int32, (1, width), 1)
    own_lane = jnp.where((lane >= HALO) & (lane < HALO + cols), 1.0, 0.0)

    def misfits(surface):
        misfit = 2.0 * gau_pad[...] * surface
        return misfit, fold_lanes(fold(misfit * surface) * own_lane)

    misfit = 2.0 * gau_pad[...] * obs_tile[...]
    copies = strips(0, *adjoint_edges(misfit))

    @pl.when(lat >= 0)
    def _():
        adjoint(2.0 * gau_pad[...] * obs_tile[...])

    for copy in copies:
        copy.wait()
    right = joined(0)

    surface = forward(right)
    surface_ref[...] = surface
    heads, tails = adjoint_edges(2.0 * gau_pad[...] * surface)
    for k in range(LEVELS):
        n = heights[k]
        for tile, x, ok, own_rows in (
            (heads, right[k][:8], valid[k][:8], above),
            (tails, right[k][n - 8 :], valid[k][n - 8 :], ~above),
        ):
            tile[k] = tile[k] + SCALES[k] * stencil(stencil(jnp.where(own_rows, x, 0.0)) * ok)
    copies = strips(1, heads, tails)
    for k in range(LEVELS):
        right_ref[k][...] = right[k]

    @pl.when(lat >= 0)
    def _():
        misfit, mu1 = misfits(surface_ref[...])
        adjoint(misfit)
        for k in range(LEVELS):
            x = right_ref[k][...]
            n = heights[k]
            head, tail = jnp.where(above, x[:8], 0.0), jnp.where(above, 0.0, x[n - 8 :])
            own_x = jnp.concatenate([head, x[8 : n - 8], tail], axis=0)
            part_ref[k][...] += SCALES[k] * stencil(stencil(own_x) * valid[k])
        mu_ref[1] = mu1

    for copy in copies:
        copy.wait()
    image = joined(1)

    surface = forward(image)
    mu0, mu1 = jnp.zeros((8, 128), F32), mu_ref[1]
    mu2 = jnp.zeros((8, 128), F32)
    _, mu3 = misfits(surface)
    for k in range(LEVELS):
        x = right_ref[k][...]
        mu0 = mu0 + squares(k, x)
        mu1 = mu1 + SCALES[k] * squares(k, stencil(x) * valid[k])
        mu2 = mu2 + squares(k, image[k])
        mu3 = mu3 + SCALES[k] * squares(k, stencil(image[k]) * valid[k])

    sub8 = lax.broadcasted_iota(jnp.int32, (8, 128), 0)
    lane8 = lax.broadcasted_iota(jnp.int32, (8, 128), 1)

    def reduce_start(stage, value, dst, sem, order, peer_of):
        red_src[stage] = value
        for d in order:
            pltpu.make_async_remote_copy(
                src_ref=red_src.at[stage],
                dst_ref=dst.at[d - 1],
                send_sem=sem.at[0],
                recv_sem=sem.at[1],
                device_id=peer_of(d),
                device_id_type=MESH,
            ).start()

    def reduce_end(value, dst, sem):
        pltpu.make_async_copy(dst, dst, sem.at[1]).wait()
        return value + jnp.sum(dst[...], axis=0)

    gathered = jnp.zeros((8, 128), F32)
    for i, value in enumerate((mu0, mu1, mu2, mu3)):
        gathered = gathered + jnp.where(sub8 == i, jnp.sum(value, axis=0, keepdims=True), 0.0)
    gathered = jnp.sum(gathered, axis=1, keepdims=True)
    moments = jnp.sum(jnp.where(sub8 == lane8, gathered, 0.0), axis=0, keepdims=True)
    reduce_start(0, moments, red_plane, plane_sem, plane, plane_peer)
    swath_src[0] = surface_ref[:, HALO : HALO + cols]
    send_swaths(0)
    swath_src[1] = surface[:, HALO : HALO + cols]
    for k in range(LEVELS):
        r_out[k][...] = extract(k, right_ref[k][...])
        q_out[k][...] = extract(k, image[k])
    moments = reduce_end(moments, red_plane, plane_sem)
    pl.semaphore_wait(line_ready, 2)
    reduce_start(1, moments, red_line, line_sem, line, line_peer)
    send_swaths(1)
    everything = swath_dst.at[0, :, : (n_lon - 1) * cols]
    for which, out in ((0, first_out), (1, second_out)):
        pltpu.make_async_copy(everything, everything, swath_sem.at[2 * which + 1]).wait()
        out[...] = swath_dst[which]
    moments = reduce_end(moments, red_line, line_sem)

    m0, m1, m2, m3 = (moments[:, i : i + 1] for i in range(4))
    alpha = m0 / m1
    grow = alpha * m2 / m1
    second_norm = alpha * alpha * m2 - m0
    curv = alpha * alpha * m3 - grow * grow * m1
    gamma = second_norm / curv
    lane1 = lane8[:1]
    mix_out[...] = jnp.where(lane1 == 0, alpha + gamma * grow, 0.0) + jnp.where(lane1 == 1, -alpha * gamma, 0.0)

    for which in range(2):
        pltpu.make_async_copy(everything, everything, swath_sem.at[2 * which]).wait()
    pltpu.make_async_copy(red_plane, red_plane, plane_sem.at[0]).wait()
    pltpu.make_async_copy(red_line, red_line, line_sem.at[0]).wait()


def combine(*refs):
    mix = refs[0][...]
    a, b = mix[:, 0:1], mix[:, 1:2]
    count = LEVELS + 1
    for first, second, out in zip(refs[1 : 1 + count], refs[1 + count : 1 + 2 * count], refs[1 + 2 * count :]):
        out[...] = a * first[...] + b * second[...]


def body(observed, gauged):
    n_lat, n_lon = lax.axis_size("lat"), lax.axis_size("lon")
    rows, cols = gauged.shape
    swath = observed.shape[0]
    width = cols + 2 * HALO
    back, edge, spread, table = tables(rows, cols)
    level_shapes = [jax.ShapeDtypeStruct((rows // s, cols // s), F32) for s in SPACINGS]
    swath_shape = jax.ShapeDtypeStruct(observed.shape, F32)
    node_shapes = [pltpu.VMEM((rows // s + 2 * MARGIN, lanes_of(width, s)), F32) for s in SPACINGS]
    vmem = pl.BlockSpec(memory_space=pltpu.VMEM)
    anywhere = pl.BlockSpec(memory_space=pl.ANY)
    dma = pltpu.SemaphoreType.DMA
    *pieces, mix = pl.pallas_call(
        functools.partial(kernel, n_lat, n_lon),
        out_shape=[pltpu.VMEM(x.shape, F32) for x in (*level_shapes, *level_shapes, swath_shape, swath_shape)]
        + [pltpu.VMEM((1, 128), F32)],
        in_specs=[anywhere] * 6,
        out_specs=[vmem] * 11,
        scratch_shapes=[
            pltpu.VMEM(observed.shape, F32),
            pltpu.VMEM(gauged.shape, gauged.dtype),
            pltpu.VMEM(back.shape, BF16),
            pltpu.VMEM(edge.shape, BF16),
            pltpu.VMEM(spread.shape, BF16),
            pltpu.VMEM(table.shape, BF16),
            pltpu.VMEM((swath, n_lon * cols + 2 * HALO), F32),
            pltpu.VMEM((rows, width), F32),
            pltpu.VMEM((rows, width), F32),
            pltpu.VMEM((2, rows // 2, 128), F32),
            pltpu.VMEM((2, rows // 2, 128), F32),
            pltpu.VMEM((rows + 2 * MARGIN, width), F32),
            *node_shapes,
            *node_shapes,
            pltpu.VMEM((rows, width), F32),
            pltpu.VMEM((2, 8, 128), F32),
            *[pltpu.VMEM((2, 2, 8, sum(lanes_of(width, s) for s in SPACINGS[:3])), F32)] * 2,
            pltpu.VMEM((2, rows, cols), F32),
            pltpu.VMEM((2, swath, n_lon * cols), F32),
            pltpu.VMEM((2, 1, 128), F32),
            pltpu.VMEM((2 * n_lon - 1, 1, 128), F32),
            pltpu.VMEM((n_lat // 2 - 1, 1, 128), F32),
            dma((6,)),
            dma((2,)),
            dma((4,)),
            dma((8,)),
            dma((4,)),
            dma((2,)),
            dma((2,)),
            pltpu.SemaphoreType.REGULAR,
        ],
        compiler_params=pltpu.CompilerParams(collective_id=0, has_side_effects=True),
        name="krylov",
    )(observed, gauged, back, edge, spread, table)
    mix, *pieces = [pltpu.with_memory_space_constraint(x, pltpu.VMEM) for x in (mix, *pieces)]
    firsts = [*pieces[:LEVELS], pieces[2 * LEVELS]]
    seconds = [*pieces[LEVELS : 2 * LEVELS], pieces[2 * LEVELS + 1]]
    return pl.pallas_call(
        combine,
        out_shape=(*level_shapes, swath_shape),
        in_specs=[vmem] * 11,
        out_specs=[vmem] * 5,
        name="combine",
    )(mix, *firsts, *seconds)


def solution(mesh):
    tile = P("lat", "lon")
    swaths = P(("lat", "lon"), None)
    return jax.shard_map(
        body,
        mesh=mesh,
        in_specs=(swaths, tile),
        out_specs=(tile, tile, tile, tile, swaths),
        check_vma=False,
    )
```
